32 devices in a mesh: ex: 4 (over z), ey: 2 (over y), ez: 4 (over x, core).
Axes of the slice: x: 2, y: 2, z: 4, core: 2. Of those that a mesh axis runs over, the one named last changes fastest.
Arguments:
- residual: float32 [64, 32, 512], P('ez', 'ey', 'ex'), may hold values from -6 to 6
- local_stream: float32 [18, 18], replicated, may hold values from -1.5 to 1.5
- local_normal: float32 [2, 18, 18], P('ey'), may hold values from -1.5 to 1.5
- local_span: float32 [18, 18], replicated, may hold values from -1.5 to 1.5
- eigen_stream: float32 [18], replicated, may hold values from 0.3 to 3
- eigen_normal: float32 [2, 18], P('ey'), may hold values from 0.3 to 3
- eigen_span: float32 [18], replicated, may hold values from 0.3 to 3
- vertex_stream: float32 [32, 32], replicated, may hold values from -1 to 1
- vertex_normal: float32 [2, 2], replicated, may hold values from -4 to 4
- vertex_span: float32 [4, 4], replicated, may hold values from -3 to 3
- level_stream: float32 [32], replicated, may hold values from 4 to 40
- level_normal: float32 [2], replicated, may hold values from 4 to 40
- level_span: float32 [4], replicated, may hold values from 4 to 40
Outputs:
- applied: float32 [64, 32, 512], P('ez', 'ey', 'ex')
The draws below stay inside these ranges and needn't reach their ends.
All inputs are finite; a program needn't handle non-finite values.
Results may differ from the reference program's by a relative error of at most 0.0003.
Values sent between devices are 32-bit elements; how exact they have to be, the bound alone decides.
A program may use at most 64 MiB of HBM per device.

```python
import math
import jax
import jax.numpy as jnp
from jax import lax

NODES = 16
BLOCK = 18
EX_TOT = 32
EY_TOT = 2
EZ_TOT = 4
XP = 512
YP = 32
ZP = 64


def block_scale(stream_key, extent, cuts, smallest, top_value):
    def one(position, blocks):
        draws = jax.random.uniform(jax.random.fold_in(jax.random.fold_in(stream_key, 6), position), (blocks,), jnp.float32, smallest / len(cuts), top_value / len(cuts))
        return jnp.repeat(jnp.exp(draws), extent[position] // blocks).reshape((-1,) + (1,) * (len(extent) - position - 1))

    level = one(*cuts[0])
    for cut in cuts[1:]:
        level = level * one(*cut)
    return level


def centred(stream_key, dims, scale, reach, shards=(), held_as=jnp.bfloat16):
    array = scale * jax.random.normal(stream_key, dims, jnp.float32)
    if shards:
        array = array * block_scale(stream_key, dims, shards, -0.22, 0.18)
    return jnp.clip(array, -reach, reach).astype(held_as)


def setup_inputs(seed: int = 0) -> dict:
    arg_keys = jax.random.split(jax.random.key(seed), 14)
    return {
        "residual": centred(arg_keys[0], (ZP, YP, XP), 1.0, 6.0, ((0, 4), (1, 2), (2, 4)), jnp.float32),
        "local_stream": centred(arg_keys[1], (BLOCK, BLOCK), BLOCK ** -0.5, 1.5, (), jnp.float32),
        "local_normal": centred(arg_keys[2], (EY_TOT, BLOCK, BLOCK), BLOCK ** -0.5, 1.5, ((0, 2),), jnp.float32),
        "local_span": centred(arg_keys[3], (BLOCK, BLOCK), BLOCK ** -0.5, 1.5, (), jnp.float32),
        "eigen_stream": jnp.clip(jnp.exp(jax.random.uniform(arg_keys[4], (BLOCK,), jnp.float32, math.log(0.3), math.log(3.0))), 0.3, 3.0),
        "eigen_normal": jnp.clip(jnp.exp(math.log(3.0) - 2.3025851 * jax.random.uniform(arg_keys[5], (EY_TOT, BLOCK), jnp.float32) ** block_scale(arg_keys[5], (EY_TOT, BLOCK), ((0, 2),), -0.2, 0.2)), 0.3, 3.0),
        "eigen_span": jnp.clip(jnp.exp(jax.random.uniform(arg_keys[6], (BLOCK,), jnp.float32, math.log(0.3), math.log(3.0))), 0.3, 3.0),
        "vertex_stream": centred(arg_keys[7], (EX_TOT, EX_TOT), EX_TOT ** -0.5, 1.0, (), jnp.float32),
        "vertex_normal": centred(arg_keys[8], (EY_TOT, EY_TOT), EY_TOT ** -0.5, 4.0, (), jnp.float32),
        "vertex_span": centred(arg_keys[9], (EZ_TOT, EZ_TOT), EZ_TOT ** -0.5, 3.0, (), jnp.float32),
        "level_stream": jnp.clip(jnp.exp(jax.random.uniform(arg_keys[10], (EX_TOT,), jnp.float32, math.log(4.0), math.log(40.0))), 4.0, 40.0),
        "level_normal": jnp.clip(jnp.exp(jax.random.uniform(arg_keys[11], (EY_TOT,), jnp.float32, math.log(4.0), math.log(40.0))), 4.0, 40.0),
        "level_span": jnp.clip(jnp.exp(jax.random.uniform(arg_keys[12], (EZ_TOT,), jnp.float32, math.log(4.0), math.log(40.0))), 4.0, 40.0),
    }


HIGHEST = lax.Precision.HIGHEST


def corner_weights(points):
    nodes_at = -jnp.cos(jnp.pi * jnp.arange(points, dtype=jnp.float32) / (points - 1))
    return jnp.stack([(1.0 - nodes_at) / 2.0, (1.0 + nodes_at) / 2.0], axis=1)


def split_windows(values, number):
    points = (values.shape[-1] - 2) // number
    inside = values[..., 1:-1].reshape(values.shape[:-1] + (number, points))
    lower_rim = values[..., 0:points * number:points][..., None]
    upper_rim = values[..., points + 1::points][..., None]
    return jnp.concatenate([lower_rim, inside, upper_rim], axis=-1)


def merge_windows(blocks, number):
    points = blocks.shape[-1] - 2
    inside = blocks[..., 1:-1].reshape(blocks.shape[:-2] + (number * points,))
    padded = jnp.pad(inside, [(0, 0)] * (inside.ndim - 1) + [(1, 1)])
    padded = padded.at[..., 0:points * number:points].add(blocks[..., 0])
    padded = padded.at[..., points + 1::points].add(blocks[..., -1])
    return padded


def local_solve(blocks, stream, normal, span, eig_stream, eig_normal, eig_span):
    modal = jnp.einsum('aibjck,ip->apbjck', blocks, stream, precision=HIGHEST)
    modal = jnp.einsum('apbjck,bjq->apbqck', modal, normal, precision=HIGHEST)
    modal = jnp.einsum('apbqck,kr->apbqcr', modal, span, precision=HIGHEST)
    divisor = (eig_stream[None, :, None, None, None, None] + eig_normal[None, None, :, :, None, None]
               + eig_span[None, None, None, None, None, :])
    modal = modal / divisor
    modal = jnp.einsum('apbqcr,kr->apbqck', modal, span, precision=HIGHEST)
    modal = jnp.einsum('apbqck,bjq->apbjck', modal, normal, precision=HIGHEST)
    return jnp.einsum('apbjck,ip->aibjck', modal, stream, precision=HIGHEST)


def restrict(shaped, weights):
    partial_sum = jnp.einsum('zkyjxi,ia->zkyjxa', shaped, weights, precision=HIGHEST)
    partial_sum = jnp.einsum('zkyjxa,jb->zkybxa', partial_sum, weights, precision=HIGHEST)
    return jnp.einsum('zkybxa,kc->zcybxa', partial_sum, weights, precision=HIGHEST)


def prolong(corner_vals, weights):
    partial_sum = jnp.einsum('zcybxa,ia->zcybxi', corner_vals, weights, precision=HIGHEST)
    partial_sum = jnp.einsum('zcybxi,jb->zcyjxi', partial_sum, weights, precision=HIGHEST)
    return jnp.einsum('zcyjxi,kc->zkyjxi', partial_sum, weights, precision=HIGHEST)


def fold_periodic(values):
    inside = values[..., 1:-1]
    inside = inside.at[..., 0].add(values[..., -1])
    return inside.at[..., -1].add(values[..., 0])


def reference(residual, local_stream, local_normal, local_span, eigen_stream, eigen_normal, eigen_span,
              vertex_stream, vertex_normal, vertex_span, level_stream, level_normal, level_span):
    points = NODES
    padded = jnp.pad(residual, ((1, 1), (0, 0), (1, 1)), mode="wrap")
    padded = jnp.pad(padded, ((0, 0), (1, 1), (0, 0)))

    def one_layer(layer_index):
        slab_values = lax.dynamic_slice_in_dim(padded, layer_index * points, points + 2, 0)
        blocks = split_windows(slab_values, EX_TOT)
        blocks = jnp.moveaxis(blocks, 1, -1)
        blocks = split_windows(blocks, EY_TOT)
        blocks = jnp.moveaxis(blocks, 0, -1)[..., None, :]
        solved = local_solve(blocks, local_stream, local_normal, local_span,
                             eigen_stream, eigen_normal, eigen_span)[..., 0, :]
        solved = jnp.moveaxis(solved, -1, 0)
        solved = merge_windows(solved, EY_TOT)
        solved = jnp.moveaxis(solved, -1, 1)
        return merge_windows(solved, EX_TOT)

    layers = lax.map(one_layer, jnp.arange(EZ_TOT, dtype=jnp.int32))
    layers = jnp.moveaxis(layers, (0, 1), (-2, -1))
    gathered = jnp.moveaxis(merge_windows(layers, EZ_TOT), -1, 0)
    schwarz = fold_periodic(gathered)
    schwarz = jnp.moveaxis(fold_periodic(jnp.moveaxis(schwarz, 0, -1)), -1, 0)
    schwarz = schwarz[:, 1:-1, :]

    weights = corner_weights(points)
    shaped = residual.reshape(EZ_TOT, points, EY_TOT, points, EX_TOT, points)
    corner = restrict(shaped, weights)
    loads_x = corner[..., 0] + jnp.roll(corner[..., 1], 1, axis=-1)
    lower_part = loads_x[:, :, :, 0, :]
    upper_part = jnp.concatenate([jnp.zeros_like(loads_x[:, :, :1, 1, :]), loads_x[:, :, :-1, 1, :]], axis=2)
    loads_y = lower_part + upper_part
    loads = loads_y[:, 0] + jnp.roll(loads_y[:, 1], 1, axis=0)
    modes = jnp.einsum('zyx,xp->zyp', loads, vertex_stream, precision=HIGHEST)
    modes = jnp.einsum('zyp,yn->znp', modes, vertex_normal, precision=HIGHEST)
    modes = jnp.einsum('znp,zm->mnp', modes, vertex_span, precision=HIGHEST)
    scaled = modes / (level_span[:, None, None] + level_normal[None, :, None] + level_stream[None, None, :])
    coarse = jnp.einsum('mnp,zm->znp', scaled, vertex_span, precision=HIGHEST)
    coarse = jnp.einsum('znp,yn->zyp', coarse, vertex_normal, precision=HIGHEST)
    coarse = jnp.einsum('zyp,xp->zyx', coarse, vertex_stream, precision=HIGHEST)
    extended = jnp.concatenate([coarse, coarse[:1]], axis=0)
    extended = jnp.concatenate([extended, jnp.zeros_like(extended[:, :1])], axis=1)
    extended = jnp.concatenate([extended, extended[:, :, :1]], axis=2)
    pairs_x = jnp.stack([extended[..., :-1], extended[..., 1:]], axis=-1)
    pairs_y = jnp.stack([pairs_x[:, :-1], pairs_x[:, 1:]], axis=2)
    pairs_z = jnp.stack([pairs_y[:-1], pairs_y[1:]], axis=1)
    correction = prolong(pairs_z, weights).reshape(ZP, YP, XP)
    return schwarz + correction
```

```python
import functools
import math

import jax
import jax.numpy as jnp
from jax import lax
from jax.experimental import pallas as pl
from jax.experimental.pallas import tpu as pltpu
from jax.sharding import PartitionSpec as P

F32 = jnp.float32
BF16 = jnp.bfloat16
I32 = jnp.int32
DIRS = ((1, 0), (-1, 0), (0, 1), (0, -1), (1, 1), (1, -1), (-1, 1), (-1, -1))


def iota(shape, dim):
    return lax.broadcasted_iota(I32, shape, dim)


def quotient(x, d):
    return (x * (65536 // d + 1)) >> 16


def onehot(mask):
    return jnp.where(mask, 1.0, 0.0).astype(F32)


def split(x):
    hi = x.astype(BF16)
    return hi, (x - hi.astype(F32)).astype(BF16)


def dg(a, b, dims):
    return lax.dot_general(a, b, ((dims[:1], dims[1:]), ((), ())), preferred_element_type=F32)


def dot3(a, b, dims=(1, 0)):
    (ah, al), (bh, bl) = a, b
    return dg(ah, bh, dims) + (dg(ah, bl, dims) + dg(al, bh, dims))


def pick(mask, values, dims=(1, 0)):
    hi, lo = split(values)
    mask = mask.astype(BF16)
    return dg(mask, hi, dims) + dg(mask, lo, dims)


def hat(index, points):
    out = jnp.zeros(index.shape, F32)
    for i in range(points):
        out = jnp.where(index == i, (1.0 - math.cos(math.pi * i / (points - 1))) / 2.0, out)
    return out


def kernel(sizes, *refs):
    inputs, out = refs[:13], refs[13]
    (
        rim, got, face, xp, xg, xr, gx, tg, gr, kh, kl, us, back, mine, parts, ssem, rsem, isem,
    ) = refs[14:32]
    held = refs[32:]
    (
        res, stream, normal, span, eig_x, eig_y, eig_z,
        v_stream, v_normal, v_span, lev_x, lev_y, lev_z,
    ) = held
    nx, ny, nz = sizes
    block = stream.shape[0]
    n = block - 2
    sh = n.bit_length() - 1
    length = res.shape[2]
    ne = length // n
    main = n * n
    edge = main + 4 * n
    nrim = rim.shape[0]
    rows, lanes = kh.shape
    nv, nm = v_stream.shape
    mn = nz * ny
    ix, iy, iz = lax.axis_index("ex"), lax.axis_index("ey"), lax.axis_index("ez")

    def fetch(i):
        return pltpu.make_async_copy(inputs[i], held[i], isem.at[i])

    for ref in (rim, got, xg, xr, tg, gr):
        ref[...] = jnp.zeros_like(ref)

    def wrap(i, size):
        return lax.rem(i + size, size)

    def where(dx, dy, dz):
        at = {}
        if dx:
            at["ex"] = wrap(ix + dx, nx)
        if dy:
            at["ey"] = iy + dy
        if dz:
            at["ez"] = wrap(iz + dz, nz)
        return at

    def has(dy):
        return jnp.logical_and(iy + dy >= 0, iy + dy < ny)

    def by_y(fn):
        fn(0)
        for dy in (1, -1):
            pl.when(has(dy))(functools.partial(fn, dy))

    barrier = pltpu.get_barrier_semaphore()

    def signal(at):
        pl.semaphore_signal(
            barrier, inc=1, device_id=at, device_id_type=pl.DeviceIdType.MESH
        )

    def greet(dy):
        for dx in (1, -1, 0):
            for dz in (1, -1, 0):
                if dx or dy or dz:
                    signal(where(dx, dy, dz))

    groups = (("ez", "ey"), ("ex",)) if mn <= 16 else (("ez",), ("ey",), ("ex",))

    def peers(axes):
        found = []
        for d in range(nz if "ez" in axes else 1):
            for f in range(ny if "ey" in axes else 1):
                for e in range(nx if "ex" in axes else 1):
                    at = {}
                    if d:
                        at["ez"] = lax.rem(iz + d, nz)
                    if f:
                        at["ey"] = lax.rem(iy + f, ny)
                    if e:
                        at["ex"] = lax.rem(ix + e, nx)
                    near = d in (0, 1, nz - 1) and e in (0, 1, nx - 1) and f < (2 if ny == 2 else 1)
                    if at:
                        found.append((at, near))
        return found

    by_y(greet)
    greeted = 8 + jnp.where(iy > 0, 9, 0) + jnp.where(iy < ny - 1, 9, 0)
    for axes in groups:
        for at, near in peers(axes):
            if not near:
                signal(at)
                greeted = greeted + 1
    for i in range(13):
        fetch(i).start()

    def shipped(src, dst, slot, at):
        return pltpu.make_async_remote_copy(
            src_ref=src, dst_ref=dst, send_sem=ssem.at[slot], recv_sem=rsem.at[slot],
            device_id=at, device_id_type=pl.DeviceIdType.MESH,
        )

    def span_of(dz, dy):
        if dy == 0:
            return (0 if dz > 0 else n), n
        if dz == 0:
            return (2 * n if dy > 0 else 3 * n), n
        return 4 * n + (0 if dz > 0 else 2) + (0 if dy > 0 else 1), 1

    def halo(s):
        dz, dy = DIRS[s]
        if dy == 0:
            src = res.at[n - 1 if dz > 0 else 0]
        elif dz == 0:
            src = res.at[:, n - 1 if dy > 0 else 0]
        else:
            src = res.at[n - 1 if dz > 0 else 0, pl.ds(n - 1 if dy > 0 else 0, 1)]
        at, number = span_of(dz, dy)
        return shipped(src, rim.at[pl.ds(at, number)], (0, 1, 2)[dy], where(0, dy, dz))

    def ret(s):
        dz, dy = DIRS[s]
        part = pl.ds(*span_of(-dz, -dy))
        return shipped(back.at[part], got.at[part], 3 + (0, 1, 2)[dy], where(0, dy, dz))

    def halos(dy):
        return [halo(s) for s in range(8) if DIRS[s][1] == dy]

    def rets(dy):
        return [ret(s) for s in range(8) if DIRS[s][1] == dy]

    def planes(src, whole, rest, base, dy):
        copies = []
        for dx in (1, -1):
            near, far = (8, 0) if dx > 0 else (0, 8)
            for s, (dz, sy) in enumerate(DIRS):
                if sy == dy:
                    copies.append(shipped(
                        src.at[pl.ds(near, 1), pl.ds(main, rows - main)],
                        rest.at[pl.ds(far + s, 1)], base + (0, 1, 2)[dy], where(dx, dy, dz),
                    ))
            if dy == 0:
                copies.append(shipped(
                    src.at[pl.ds(near, 1), pl.ds(0, main)],
                    whole.at[pl.ds(far, 1), pl.ds(0, main)], base, where(dx, 0, 0),
                ))
        return copies

    def start(make):
        def go(dy):
            for c in make(dy):
                c.start()

        by_y(go)

    def take(sem, ref, count):
        bulk = ref.at[pl.ds(0, count)]
        pltpu.make_async_copy(bulk, bulk, sem).wait()

    amounts = {
        0: (rim, 2 * n, n + 2), 3: (got, 2 * n, n + 2),
        6: (xr, 4 + 2 * main // (rows - main), 6), 9: (gr, 4 + 2 * main // (rows - main), 6),
    }

    def sent(base):
        ref, level, slope = amounts[base]
        by_y(lambda dy: take(ssem.at[base + (0, 1, 2)[dy]], ref, slope if dy else level))

    def received(base):
        ref, level, slope = amounts[base]
        by_y(lambda dy: take(rsem.at[base + (0, 2, 1)[dy]], ref, slope if dy else level))

    def exchange(k):
        before = sum(len(peers(axes)) for axes in groups[:k])
        return [
            shipped(mine.at[k], parts.at[before + i], 12 + before + i, at)
            for i, (at, _) in enumerate(peers(groups[k]))
        ]

    def gather(k):
        before = sum(len(peers(axes)) for axes in groups[:k])
        total = mine[k]
        for i, c in enumerate(exchange(k)):
            c.wait_recv()
            total = total + parts[before + i]
        return total

    def begin(k):
        for c in exchange(k):
            c.start()

    hrow, hcol = iota((8, main), 0), iota((8, main), 1)
    wk, wj = hat(hcol >> sh, n), hat(hcol & (n - 1), n)
    hyz = jnp.where((hrow & 2) > 0, wk, 1.0 - wk) * jnp.where((hrow & 1) > 0, wj, 1.0 - wj)
    hyz = split(jnp.where(hrow < 4, hyz, 0.0))
    xrow, xcol = iota((length, nv), 0), iota((length, nv), 1)
    wx = hat(xrow & (n - 1), n)
    first_el = ix * ne + (xrow >> sh)
    after = jnp.where(first_el + 1 >= nv, first_el + 1 - nv, first_el + 1)
    hatx = jnp.where(xcol == first_el, 1.0 - wx, 0.0) + jnp.where(xcol == after, wx, 0.0)
    hatx = split(hatx)
    mrow, mcol = iota((mn, nz), 0), iota((mn, nz), 1)
    is_m = onehot((mrow >= mcol * ny) & (mrow < (mcol + 1) * ny))
    nrow, ncol = iota((mn, ny), 0), iota((mn, ny), 1)
    is_n = onehot(nrow - ny * quotient(nrow, ny) == ncol)
    vrow, vcol = iota((nz, 8), 0), iota((nz, 8), 1)
    vz = iz + (vcol >> 1)
    vz = jnp.where(vz >= nz, vz - nz, vz)
    at_z = onehot((vrow == vz) & (vcol < 4))
    urow, ucol = iota((ny, 8), 0), iota((ny, 8), 1)
    at_y = onehot((urow == iy + (ucol & 1)) & (ucol < 4))
    orow, ocol = iota((16, length), 0), iota((16, length), 1)
    ends = onehot(((orow == 0) & (ocol == 0)) | ((orow == 8) & (ocol == length - 1))).astype(BF16)
    face[...] = jnp.zeros_like(face)
    mine[...] = jnp.zeros_like(mine)

    for i in range(13):
        fetch(i).wait()
    data = res[...].reshape(main, length)
    d_split = split(data)
    face[0:n] = res[n - 1]
    face[n : 2 * n] = res[0]
    face[2 * n : 3 * n] = res[:, n - 1]
    face[3 * n : 4 * n] = res[:, 0]
    for e in range(4):
        k, j = (n - 1, 0)[e >> 1], (n - 1, 0)[e & 1]
        face[4 * n + e : 4 * n + e + 1] = res[k, j : j + 1]
    f_split = split(face[...])
    xp[:, :main] = dg(ends, d_split[0], (1, 1)) + dg(ends, d_split[1], (1, 1))
    xp[:, main:] = dg(ends, f_split[0], (1, 1)) + dg(ends, f_split[1], (1, 1))
    wxm = split(dot3(hatx, split(v_stream[...])))
    amat = pick(is_m, dot3(split(v_span[...].T), split(at_z)))
    amat = amat * pick(is_n, dot3(split(v_normal[...].T), split(at_y)))
    loads = dot3(split(dot3(hyz, d_split)), wxm)
    mine[0, :, :nm] = dot3(split(amat), split(loads))

    pl.semaphore_wait(barrier, greeted)
    start(lambda dy: planes(xp, xg, xr, 6, dy))
    start(halos)
    begin(0)

    row, col = iota((rows, block), 0), iota((rows, block), 1)
    low = row & (n - 1)
    e0 = row - edge
    rk = jnp.where(row < main, (row >> sh) + 1, low + 1)
    rk = jnp.where((row >= main) & (row < main + n), 0, rk)
    rk = jnp.where((row >= main + n) & (row < main + 2 * n), n + 1, rk)
    rk = jnp.where(row >= edge, jnp.where(e0 < 2, 0, n + 1), rk)
    rk = jnp.where(row >= edge + 4, -1, rk)
    rj = jnp.where((row >= main + 2 * n) & (row < main + 3 * n), 0, low + 1)
    rj = jnp.where((row >= main + 3 * n) & (row < main + 4 * n), n + 1, rj)
    rj = jnp.where(row >= edge, jnp.where((e0 & 1) == 0, 0, n + 1), rj)
    rj = jnp.where(row >= edge + 4, -1, rj)
    sel_k, sel_j = onehot(rk == col), onehot(rj == col)
    brow, bcol = iota((block, lanes), 0), iota((block, lanes), 1)
    bq = quotient(bcol, block)
    to_r = onehot(bq == brow)
    to_q = onehot((bcol - block * bq == brow) & (bcol < block * block))
    span_l = dot3(split(span[...]), split(to_r))
    normal_l = dot3(split(normal[...].reshape(block, block)), split(to_q))
    kmat = pick(sel_k, span_l) * pick(sel_j, normal_l)
    k_hi, k_lo = split(kmat)
    kh[...] = k_hi
    kl[...] = k_lo
    k_all = kh[...], kl[...]
    k_main = kh[0:main], kl[0:main]
    k_rim = kh[main : main + nrim], kl[main : main + nrim]

    nep = length + 16
    pairs = ne * block
    npad = -(-pairs // 16) * 16

    def place(c):
        far = jnp.where(c == length + 8, length, -n * length)
        return jnp.where(c < length, c, jnp.where(c == length, -1, far))

    wrow, wcol = iota((npad, nep), 0), iota((npad, nep), 1)
    xi = place(wcol) + 1 - n * quotient(wrow, block)
    trow, tcol = iota((block, nep), 0), iota((block, nep), 1)
    tx = place(tcol)
    tm = (tx + 1) & (n - 1)
    s_t = split(stream[...].T)
    first = dot3(s_t, split(onehot(trow == tm)))
    second = dot3(s_t, split(onehot(trow - n == tm)))
    prow, pcol = iota((npad, block), 0), iota((npad, block), 1)
    is_p = onehot((prow - block * quotient(prow, block) == pcol) & (prow < pairs))
    wmat = jnp.where((xi >= 0) & (xi < n), pick(is_p, first), 0.0)
    wmat = wmat + jnp.where((xi >= n) & (xi < block), pick(is_p, second), 0.0)
    w_h, w_l = split(wmat[:, :length])
    w_in = jnp.concatenate([w_h, ends], axis=0), jnp.concatenate([w_l, jnp.zeros_like(ends)], axis=0)
    w_back = split(wmat.T)
    eig_yz = dot3(split(jnp.broadcast_to(eig_z[...], (8, block))), split(to_r))
    eig_yz = eig_yz + dot3(split(jnp.broadcast_to(eig_y[...], (8, block))), split(to_q))
    ecol = jnp.sum(is_p * eig_x[...], axis=1, keepdims=True)
    ecol = jnp.where(iota((npad, 1), 0) < pairs, ecol, 1.0)
    inverse = 1.0 / (ecol + eig_yz[0:1])
    from_left = dot3(w_back, split(wmat[:, length : length + 1] * inverse))
    from_right = dot3(w_back, split(wmat[:, length + 8 : length + 9] * inverse))
    own_left = from_left[length : length + 1]
    own_right = from_right[length + 8 : length + 9]
    level = jnp.sum(is_m * lev_z[...], axis=1, keepdims=True)
    level = level + jnp.sum(is_n * lev_y[...], axis=1, keepdims=True) + lev_x[...]
    srow, slane = iota((8, rows - main), 0), iota((8, rows - main), 1)
    came = jnp.zeros(srow.shape, F32)
    went = jnp.zeros(srow.shape, F32)
    for s, (dz, dy) in enumerate(DIRS):
        at, number = span_of(dz, dy)
        came = jnp.where((srow == s) & (slane >= at) & (slane < at + number), 1.0, came)
        at, number = span_of(-dz, -dy)
        went = jnp.where((srow == s) & (slane >= at) & (slane < at + number), 1.0, went)
    part = dot3(split(dot3(w_in, d_split, (1, 1))), k_main)

    received(0)
    onto = dot3(w_in, split(rim[...]), (1, 1))
    part = part + dot3(split(onto), k_rim)
    both = dot3(w_back, split(part[:npad] * inverse))
    gx[...] = dot3(split(both[length:]), k_all, (1, 1))
    start(lambda dy: planes(gx, tg, gr, 9, dy))
    us[...] = both[:length]
    us[0:1] += own_right * part[npad : npad + 1]
    us[length - 1 : length] += own_left * part[npad + 8 : npad + 9]

    for k in range(len(groups) - 1):
        mine[k + 1] = gather(k)
        begin(k + 1)

    received(6)
    xg[0:1, main:] = jnp.sum(xr[0:8] * came, axis=0, keepdims=True)
    xg[8:9, main:] = jnp.sum(xr[8:16] * came, axis=0, keepdims=True)
    hx = dot3(split(xg[...]), k_all)
    u = split(us[...] + from_left[:length] * hx[0:1] + from_right[:length] * hx[8:9])
    back[...] = dot3(k_rim, u, (1, 1))
    start(rets)
    result = dot3(k_main, u, (1, 1))

    scaled = split(gather(len(groups) - 1)[:, :nm] / level)
    coarse = dot3(split(amat.T), scaled)
    coarse = dot3(split(coarse), wxm, (1, 1))
    result = result + dot3(hyz, split(coarse), (0, 0))

    received(9)
    tg[0:1, main:] = jnp.sum(gr[0:8] * went, axis=0, keepdims=True)
    tg[8:9, main:] = jnp.sum(gr[8:16] * went, axis=0, keepdims=True)
    t_h, t_l = split(tg[...])
    turned = dg(t_h, ends, (0, 0)) + dg(t_l, ends, (0, 0))
    out[...] = (result + turned[:main]).reshape(n, n, length)
    received(3)
    extra = got[...] + turned[main : main + nrim]
    out[n - 1] += extra[0:n]
    out[0] += extra[n : 2 * n]
    out[:, n - 1] += extra[2 * n : 3 * n]
    out[:, 0] += extra[3 * n : 4 * n]
    for e in range(4):
        k, j = (n - 1, 0)[e >> 1], (n - 1, 0)[e & 1]
        out[k, j : j + 1] += extra[4 * n + e : 4 * n + e + 1]
    for base in (0, 3, 6, 9):
        sent(base)
    for k in range(len(groups)):
        for c in exchange(k):
            c.wait_send()


def per_device(sizes, residual, local_stream, local_normal, local_span, eigen_stream, eigen_normal,
               eigen_span, vertex_stream, vertex_normal, vertex_span, level_stream, level_normal,
               level_span):
    nx, ny, nz = sizes
    block = local_stream.shape[0]
    n = block - 2
    length = residual.shape[2]
    nrim = 4 * n + 16
    wide = n * n + -(-nrim // 128) * 128
    lanes = -(-block * block // 128) * 128
    mn = ny * nz
    peers = mn - 1 + nx - 1 if mn <= 16 else nx + ny + nz - 3
    args = (
        residual, local_stream, local_normal.transpose(1, 0, 2), local_span,
        eigen_stream.reshape(1, -1), eigen_normal, eigen_span.reshape(1, -1), vertex_stream,
        vertex_normal, vertex_span, level_stream.reshape(1, -1), level_normal.reshape(1, -1),
        level_span.reshape(1, -1),
    )
    return pl.pallas_call(
        functools.partial(kernel, sizes),
        out_shape=pltpu.VMEM(residual.shape, F32),
        in_specs=[pl.BlockSpec(memory_space=pltpu.HBM)] * 13,
        out_specs=pl.BlockSpec(memory_space=pltpu.VMEM),
        scratch_shapes=[
            pltpu.VMEM((nrim, length), F32),
            pltpu.VMEM((nrim, length), F32),
            pltpu.VMEM((wide - n * n, length), F32),
            pltpu.VMEM((16, wide), F32),
            pltpu.VMEM((16, wide), F32),
            pltpu.VMEM((16, wide - n * n), F32),
            pltpu.VMEM((16, wide), F32),
            pltpu.VMEM((16, wide), F32),
            pltpu.VMEM((16, wide - n * n), F32),
            pltpu.VMEM((wide, lanes), BF16),
            pltpu.VMEM((wide, lanes), BF16),
            pltpu.VMEM((length, lanes), F32),
            pltpu.VMEM((nrim, length), F32),
            pltpu.VMEM((3, mn, 128), F32),
            pltpu.VMEM((peers, mn, 128), F32),
            pltpu.SemaphoreType.DMA((12 + peers,)),
            pltpu.SemaphoreType.DMA((12 + peers,)),
            pltpu.SemaphoreType.DMA((13,)),
        ] + [pltpu.VMEM(a.shape, F32) for a in args],
        compiler_params=pltpu.CompilerParams(
            collective_id=0, has_side_effects=True
        ),
    )(*args)


def solution(mesh):
    sizes = (mesh.shape["ex"], mesh.shape["ey"], mesh.shape["ez"])
    placed = (P("ez", "ey", "ex"), P(), P("ey", None, None), P(), P(), P("ey", None)) + (P(),) * 7
    return jax.shard_map(
        functools.partial(per_device, sizes), mesh=mesh, in_specs=placed,
        out_specs=P("ez", "ey", "ex"), check_vma=False,
    )
```

```python
import functools
import math

import jax
import jax.numpy as jnp
from jax import lax
from jax.experimental import pallas as pl
from jax.experimental.pallas import tpu as pltpu
from jax.sharding import PartitionSpec as P

F32 = jnp.float32
BF16 = jnp.bfloat16
I32 = jnp.int32
DIRS = ((1, 0), (-1, 0), (0, 1), (0, -1), (1, 1), (1, -1), (-1, 1), (-1, -1))


def iota(shape, dim):
    return lax.broadcasted_iota(I32, shape, dim)


def quotient(x, d):
    return (x * (65536 // d + 1)) >> 16


def onehot(mask):
    return jnp.where(mask, 1.0, 0.0).astype(F32)


def split(x):
    hi = x.astype(BF16)
    return hi, (x - hi.astype(F32)).astype(BF16)


def dg(a, b, dims):
    return lax.dot_general(a, b, ((dims[:1], dims[1:]), ((), ())), preferred_element_type=F32)


def dot3(a, b, dims=(1, 0)):
    (ah, al), (bh, bl) = a, b
    return dg(ah, bh, dims) + (dg(ah, bl, dims) + dg(al, bh, dims))


def pick(mask, values, dims=(1, 0)):
    hi, lo = split(values)
    mask = mask.astype(BF16)
    return dg(mask, hi, dims) + dg(mask, lo, dims)


def hat(index, points):
    out = jnp.zeros(index.shape, F32)
    for i in range(points):
        out = jnp.where(index == i, (1.0 - math.cos(math.pi * i / (points - 1))) / 2.0, out)
    return out


def kernel(sizes, *refs):
    inputs, out = refs[:13], refs[13]
    (
        rim, got, face, xp, xg, xr, gx, tg, gr, vv, kh, kl, k3, kth, ktl, us, back, mine, parts,
        ssem, rsem, isem,
    ) = refs[14:36]
    held = refs[36:]
    (
        res, stream, normal, span, eig_x, eig_y, eig_z,
        v_stream, v_normal, v_span, lev_x, lev_y, lev_z,
    ) = held
    nx, ny, nz = sizes
    block = stream.shape[0]
    n = block - 2
    sh = n.bit_length() - 1
    length = res.shape[2]
    ne = length // n
    main = n * n
    edge = main + 4 * n
    nrim = got.shape[0]
    rows, lanes = kh.shape
    nv, nm = v_stream.shape
    mn = nz * ny
    ix, iy, iz = lax.axis_index("ex"), lax.axis_index("ey"), lax.axis_index("ez")

    def fetch(i):
        return pltpu.make_async_copy(inputs[i], held[i], isem.at[i])

    for ref in (rim, got, xg, xr, tg.at[0:8], tg.at[length - 8 : length], gr):
        ref[...] = jnp.zeros(ref.shape, F32)

    def wrap(i, size):
        return lax.rem(i + size, size)

    def where(dx, dy, dz):
        at = {}
        if dx:
            at["ex"] = wrap(ix + dx, nx)
        if dy:
            at["ey"] = iy + dy
        if dz:
            at["ez"] = wrap(iz + dz, nz)
        return at

    def has(dy):
        return jnp.logical_and(iy + dy >= 0, iy + dy < ny)

    def by_y(fn):
        fn(0)
        for dy in (1, -1):
            pl.when(has(dy))(functools.partial(fn, dy))

    barrier = pltpu.get_barrier_semaphore()

    def signal(at):
        pl.semaphore_signal(
            barrier, inc=1, device_id=at, device_id_type=pl.DeviceIdType.MESH
        )

    def greet(dy):
        for dx in (1, -1, 0):
            for dz in (1, -1, 0):
                if dx or dy or dz:
                    signal(where(dx, dy, dz))

    groups = (("ez", "ey"), ("ex",)) if mn <= 16 else (("ez",), ("ey",), ("ex",))

    def peers(axes):
        found = []
        for d in range(nz if "ez" in axes else 1):
            for f in range(ny if "ey" in axes else 1):
                for e in range(nx if "ex" in axes else 1):
                    at = {}
                    if d:
                        at["ez"] = lax.rem(iz + d, nz)
                    if f:
                        at["ey"] = lax.rem(iy + f, ny)
                    if e:
                        at["ex"] = lax.rem(ix + e, nx)
                    near = d in (0, 1, nz - 1) and e in (0, 1, nx - 1) and f < (2 if ny == 2 else 1)
                    if at:
                        found.append((at, near))
        return found

    by_y(greet)
    greeted = 8 + jnp.where(iy > 0, 9, 0) + jnp.where(iy < ny - 1, 9, 0)
    for axes in groups:
        for at, near in peers(axes):
            if not near:
                signal(at)
                greeted = greeted + 1
    for i in range(13):
        fetch(i).start()

    def shipped(src, dst, slot, at):
        return pltpu.make_async_remote_copy(
            src_ref=src, dst_ref=dst, send_sem=ssem.at[slot], recv_sem=rsem.at[slot],
            device_id=at, device_id_type=pl.DeviceIdType.MESH,
        )

    def span_of(dz, dy):
        if dy == 0:
            return (0 if dz > 0 else n), n
        if dz == 0:
            return (2 * n if dy > 0 else 3 * n), n
        return 4 * n + (0 if dz > 0 else 2) + (0 if dy > 0 else 1), 1

    def halo(s):
        dz, dy = DIRS[s]
        if dy == 0:
            src = res.at[n - 1 if dz > 0 else 0]
        elif dz == 0:
            src = res.at[:, n - 1 if dy > 0 else 0]
        else:
            src = res.at[n - 1 if dz > 0 else 0, pl.ds(n - 1 if dy > 0 else 0, 1)]
        at, number = span_of(dz, dy)
        return shipped(src, rim.at[pl.ds(at, number)], (0, 1, 2)[dy], where(0, dy, dz))

    def ret(s):
        dz, dy = DIRS[s]
        part = pl.ds(*span_of(-dz, -dy))
        return shipped(back.at[part], got.at[part], 3 + (0, 1, 2)[dy], where(0, dy, dz))

    def halos(dy):
        return [halo(s) for s in range(8) if DIRS[s][1] == dy]

    def rets(dy):
        return [ret(s) for s in range(8) if DIRS[s][1] == dy]

    def planes(src, near_rows, whole, whole_rows, rest, base, dy):
        copies = []
        for dx in (1, -1):
            side = 0 if dx > 0 else 1
            near, far = near_rows[1 - side], 8 * side
            for s, (dz, sy) in enumerate(DIRS):
                if sy == dy:
                    copies.append(shipped(
                        src.at[pl.ds(near, 1), pl.ds(main, rows - main)],
                        rest.at[pl.ds(far + s, 1)], base + (0, 1, 2)[dy], where(dx, dy, dz),
                    ))
            if dy == 0:
                copies.append(shipped(
                    src.at[pl.ds(near, 1), pl.ds(0, main)],
                    whole.at[pl.ds(whole_rows[side], 1), pl.ds(0, main)], base, where(dx, 0, 0),
                ))
        return copies

    def start(make):
        def go(dy):
            for c in make(dy):
                c.start()

        by_y(go)

    def take(sem, ref, count):
        bulk = ref.at[pl.ds(0, count)]
        pltpu.make_async_copy(bulk, bulk, sem).wait()

    amounts = {
        0: (rim, 2 * n, n + 2), 3: (got, 2 * n, n + 2),
        6: (xr, 4 + 2 * main // (rows - main), 6), 9: (gr, 4 + 2 * main // (rows - main), 6),
    }

    def sent(base):
        ref, level, slope = amounts[base]
        by_y(lambda dy: take(ssem.at[base + (0, 1, 2)[dy]], ref, slope if dy else level))

    def received(base):
        ref, level, slope = amounts[base]
        by_y(lambda dy: take(rsem.at[base + (0, 2, 1)[dy]], ref, slope if dy else level))

    def exchange(k):
        before = sum(len(peers(axes)) for axes in groups[:k])
        return [
            shipped(mine.at[k], parts.at[before + i], 12 + before + i, at)
            for i, (at, _) in enumerate(peers(groups[k]))
        ]

    def gather(k):
        before = sum(len(peers(axes)) for axes in groups[:k])
        total = mine[k]
        for i, c in enumerate(exchange(k)):
            c.wait_recv()
            total = total + parts[before + i]
        return total

    def begin(k):
        for c in exchange(k):
            c.start()

    hrow, hcol = iota((8, main), 0), iota((8, main), 1)
    wk, wj = hat(hcol >> sh, n), hat(hcol & (n - 1), n)
    hyz = jnp.where((hrow & 2) > 0, wk, 1.0 - wk) * jnp.where((hrow & 1) > 0, wj, 1.0 - wj)
    hyz = split(jnp.where(hrow < 4, hyz, 0.0))
    xrow, xcol = iota((length, nv), 0), iota((length, nv), 1)
    wx = hat(xrow & (n - 1), n)
    first_el = ix * ne + (xrow >> sh)
    after = jnp.where(first_el + 1 >= nv, first_el + 1 - nv, first_el + 1)
    hatx = jnp.where(xcol == first_el, 1.0 - wx, 0.0) + jnp.where(xcol == after, wx, 0.0)
    hatx = split(hatx)
    mrow, mcol = iota((mn, nz), 0), iota((mn, nz), 1)
    is_m = onehot((mrow >= mcol * ny) & (mrow < (mcol + 1) * ny))
    nrow, ncol = iota((mn, ny), 0), iota((mn, ny), 1)
    is_n = onehot(nrow - ny * quotient(nrow, ny) == ncol)
    vrow, vcol = iota((nz, 8), 0), iota((nz, 8), 1)
    vz = iz + (vcol >> 1)
    vz = jnp.where(vz >= nz, vz - nz, vz)
    at_z = onehot((vrow == vz) & (vcol < 4))
    urow, ucol = iota((ny, 8), 0), iota((ny, 8), 1)
    at_y = onehot((urow == iy + (ucol & 1)) & (ucol < 4))
    orow, ocol = iota((16, length), 0), iota((16, length), 1)
    ends = onehot(((orow == 0) & (ocol == 0)) | ((orow == 8) & (ocol == length - 1))).astype(BF16)
    face[...] = jnp.zeros_like(face)
    mine[...] = jnp.zeros_like(mine)
    vv[...] = jnp.zeros_like(vv)
    tg[8 : length - 8] = jnp.zeros((length - 16, rows), F32)

    fetch(0).wait()
    data = res[...].reshape(main, length)
    d_split = split(data)
    face[0:n] = res[n - 1]
    face[n : 2 * n] = res[0]
    face[2 * n : 3 * n] = res[:, n - 1]
    face[3 * n : 4 * n] = res[:, 0]
    for e in range(4):
        k, j = (n - 1, 0)[e >> 1], (n - 1, 0)[e & 1]
        face[4 * n + e : 4 * n + e + 1] = res[k, j : j + 1]
    xp[:, :main] = data.T
    xp[:, main:] = face[...].T
    for i in range(1, 13):
        fetch(i).wait()
    wxm = split(dot3(hatx, split(v_stream[...])))
    amat = pick(is_m, dot3(split(v_span[...].T), split(at_z)))
    amat = amat * pick(is_n, dot3(split(v_normal[...].T), split(at_y)))
    loads = dot3(split(dot3(hyz, d_split)), wxm)
    mine[0, :, :nm] = dot3(split(amat), split(loads))

    pl.semaphore_wait(barrier, greeted)
    start(lambda dy: planes(xp, (0, length - 1), xg, (0, 8), xr, 6, dy))
    start(halos)
    begin(0)

    row, col = iota((rows, block), 0), iota((rows, block), 1)
    low = row & (n - 1)
    e0 = row - edge
    rk = jnp.where(row < main, (row >> sh) + 1, low + 1)
    rk = jnp.where((row >= main) & (row < main + n), 0, rk)
    rk = jnp.where((row >= main + n) & (row < main + 2 * n), n + 1, rk)
    rk = jnp.where(row >= edge, jnp.where(e0 < 2, 0, n + 1), rk)
    rk = jnp.where(row >= edge + 4, -1, rk)
    rj = jnp.where((row >= main + 2 * n) & (row < main + 3 * n), 0, low + 1)
    rj = jnp.where((row >= main + 3 * n) & (row < main + 4 * n), n + 1, rj)
    rj = jnp.where(row >= edge, jnp.where((e0 & 1) == 0, 0, n + 1), rj)
    rj = jnp.where(row >= edge + 4, -1, rj)
    sel_k, sel_j = onehot(rk == col), onehot(rj == col)
    brow, bcol = iota((block, lanes), 0), iota((block, lanes), 1)
    bq = quotient(bcol, block)
    to_r = onehot(bq == brow)
    to_q = onehot((bcol - block * bq == brow) & (bcol < block * block))
    span_l = dot3(split(span[...]), split(to_r))
    normal_l = dot3(split(normal[...].reshape(block, block)), split(to_q))
    kmat = pick(sel_k, span_l) * pick(sel_j, normal_l)
    k_hi, k_lo = split(kmat)
    kh[...] = k_hi
    kl[...] = k_lo
    wide = rows - main
    k3[0:wide] = k_hi[main:]
    k3[wide : 2 * wide] = k_hi[main:]
    k3[2 * wide :] = k_lo[main:]
    t_hi, t_lo = split(kmat.T)
    kth[...] = t_hi
    ktl[...] = t_lo
    k_main = kh[0:main], kl[0:main]

    nep = length + 16
    pairs = ne * block
    npad = -(-pairs // 16) * 16

    def place(c):
        far = jnp.where(c == length + 8, length, -n * length)
        return jnp.where(c < length, c, jnp.where(c == length, -1, far))

    wrow, wcol = iota((npad, nep), 0), iota((npad, nep), 1)
    xi = place(wcol) + 1 - n * quotient(wrow, block)
    trow, tcol = iota((block, nep), 0), iota((block, nep), 1)
    tx = place(tcol)
    tm = (tx + 1) & (n - 1)
    s_t = split(stream[...].T)
    first = dot3(s_t, split(onehot(trow == tm)))
    second = dot3(s_t, split(onehot(trow - n == tm)))
    prow, pcol = iota((npad, block), 0), iota((npad, block), 1)
    is_p = onehot((prow - block * quotient(prow, block) == pcol) & (prow < pairs))
    wmat = jnp.where((xi >= 0) & (xi < n), pick(is_p, first), 0.0)
    wmat = wmat + jnp.where((xi >= n) & (xi < block), pick(is_p, second), 0.0)
    w_h, w_l = split(wmat[:, :length])
    w_in = jnp.concatenate([w_h, ends], axis=0), jnp.concatenate([w_l, jnp.zeros_like(ends)], axis=0)
    w_two = jnp.concatenate(w_in, axis=0)
    nin = npad + 16
    cut, tail = -(-block // 16) * 16, (pairs - block) // 16 * 16
    cols = jnp.concatenate(
        [wmat[:cut, length : length + 1], wmat[tail:, length + 8 : length + 9]], axis=0
    )
    w_back = split(wmat.T)
    eig_yz = dot3(split(jnp.broadcast_to(eig_z[...], (8, block))), split(to_r))
    eig_yz = eig_yz + dot3(split(jnp.broadcast_to(eig_y[...], (8, block))), split(to_q))
    ecol = jnp.sum(is_p * eig_x[...], axis=1, keepdims=True)
    ecol = jnp.where(iota((npad, 1), 0) < pairs, ecol, 1.0)
    inverse = 1.0 / (ecol + eig_yz[0:1])
    from_left = dot3(w_back, split(wmat[:, length : length + 1] * inverse))
    from_right = dot3(w_back, split(wmat[:, length + 8 : length + 9] * inverse))
    own_left = from_left[length : length + 1]
    own_right = from_right[length + 8 : length + 9]
    level = jnp.sum(is_m * lev_z[...], axis=1, keepdims=True)
    level = level + jnp.sum(is_n * lev_y[...], axis=1, keepdims=True) + lev_x[...]
    srow, slane = iota((8, rows - main), 0), iota((8, rows - main), 1)
    came = jnp.zeros(srow.shape, F32)
    went = jnp.zeros(srow.shape, F32)
    for s, (dz, dy) in enumerate(DIRS):
        at, number = span_of(dz, dy)
        came = jnp.where((srow == s) & (slane >= at) & (slane < at + number), 1.0, came)
        at, number = span_of(-dz, -dy)
        went = jnp.where((srow == s) & (slane >= at) & (slane < at + number), 1.0, went)
    part = dot3(split(dot3(w_in, d_split, (1, 1))), k_main)

    weights = jnp.concatenate([inverse[:cut], inverse[tail:]], axis=0) * cols
    part_ends = jnp.concatenate([part[:cut], part[tail:npad]], axis=0)
    b_two = jnp.concatenate([w_back[0][:length], w_back[1][:length]], axis=0)
    spread = split(dot3(hyz, split(amat), (0, 1)))

    received(0)
    o = dg(w_two, jnp.concatenate(split(rim[...]), axis=0), (1, 1))
    onto = o[:nin, :wide] + (o[:nin, wide:] + o[nin:, :wide])
    o_h, o_l = split(onto)
    tri = jnp.concatenate([o_h, o_l, o_h], axis=1)
    tri_ends = jnp.concatenate([tri[:cut], tri[tail:npad]], axis=0)
    modal = (part_ends + dg(tri_ends, k3[...], (1, 0))) * weights
    vv[0:1] = jnp.sum(modal[:cut], axis=0, keepdims=True)
    vv[8:9] = jnp.sum(modal[cut:], axis=0, keepdims=True)
    v_h, v_l = split(vv[...])
    o = dg(jnp.concatenate([v_h, v_l], axis=0), kth[...], (1, 0))
    gx[...] = o[:16] + (o[16:] + dg(v_h, ktl[...], (1, 0)))
    start(lambda dy: planes(gx, (0, 8), tg, (0, length - 1), gr, 9, dy))

    part = part + dg(tri, k3[...], (1, 0))
    m_h, m_l = split(part[:npad] * inverse)
    o = dg(b_two, m_h, (1, 0))
    us[...] = o[:length] + (o[length:] + dg(b_two[:length], m_l, (1, 0)))
    us[0:1] += own_right * part[npad : npad + 1]
    us[length - 1 : length] += own_left * part[npad + 8 : npad + 9]

    for k in range(len(groups) - 1):
        mine[k + 1] = gather(k)
        begin(k + 1)

    received(6)
    xg[0:1, main:] = jnp.sum(xr[0:8] * came, axis=0, keepdims=True)
    xg[8:9, main:] = jnp.sum(xr[8:16] * came, axis=0, keepdims=True)
    g_h, g_l = split(xg[...])
    o = dg(jnp.concatenate([g_h, g_l], axis=0), kh[...], (1, 0))
    hx = o[:16] + (o[16:] + dg(g_h, kl[...], (1, 0)))
    u = split(us[...] + from_left[:length] * hx[0:1] + from_right[:length] * hx[8:9])
    r_two = jnp.concatenate([kh[main : main + nrim], kl[main : main + nrim]], axis=0)
    o = dg(r_two, jnp.concatenate(u, axis=0), (1, 1))
    back[...] = o[:nrim, :length] + (o[:nrim, length:] + o[nrim:, :length])
    start(rets)
    result = dot3(k_main, u, (1, 1))

    scaled = split(gather(len(groups) - 1)[:, :nm] / level)
    coarse = dot3(scaled, wxm, (1, 1))
    result = result + dot3(spread, split(coarse))

    received(9)
    tg[0:1, main:] = jnp.sum(gr[0:8] * went, axis=0, keepdims=True)
    tg[length - 1 : length, main:] = jnp.sum(gr[8:16] * went, axis=0, keepdims=True)
    turned = tg[...].T
    out[...] = (result + turned[:main]).reshape(n, n, length)
    received(3)
    extra = got[...] + turned[main : main + nrim]
    out[n - 1] += extra[0:n]
    out[0] += extra[n : 2 * n]
    out[:, n - 1] += extra[2 * n : 3 * n]
    out[:, 0] += extra[3 * n : 4 * n]
    for e in range(4):
        k, j = (n - 1, 0)[e >> 1], (n - 1, 0)[e & 1]
        out[k, j : j + 1] += extra[4 * n + e : 4 * n + e + 1]
    for base in (0, 3, 6, 9):
        sent(base)
    for k in range(len(groups)):
        for c in exchange(k):
            c.wait_send()


def per_device(sizes, residual, local_stream, local_normal, local_span, eigen_stream, eigen_normal,
               eigen_span, vertex_stream, vertex_normal, vertex_span, level_stream, level_normal,
               level_span):
    nx, ny, nz = sizes
    block = local_stream.shape[0]
    n = block - 2
    length = residual.shape[2]
    nrim = 4 * n + 16
    wide = n * n + -(-nrim // 128) * 128
    lanes = -(-block * block // 128) * 128
    mn = ny * nz
    peers = mn - 1 + nx - 1 if mn <= 16 else nx + ny + nz - 3
    args = (
        residual, local_stream, local_normal.transpose(1, 0, 2), local_span,
        eigen_stream.reshape(1, -1), eigen_normal, eigen_span.reshape(1, -1), vertex_stream,
        vertex_normal, vertex_span, level_stream.reshape(1, -1), level_normal.reshape(1, -1),
        level_span.reshape(1, -1),
    )
    return pl.pallas_call(
        functools.partial(kernel, sizes),
        out_shape=pltpu.VMEM(residual.shape, F32),
        in_specs=[pl.BlockSpec(memory_space=pltpu.HBM)] * 13,
        out_specs=pl.BlockSpec(memory_space=pltpu.VMEM),
        scratch_shapes=[
            pltpu.VMEM((wide - n * n, length), F32),
            pltpu.VMEM((nrim, length), F32),
            pltpu.VMEM((wide - n * n, length), F32),
            pltpu.VMEM((length, wide), F32),
            pltpu.VMEM((16, wide), F32),
            pltpu.VMEM((16, wide - n * n), F32),
            pltpu.VMEM((16, wide), F32),
            pltpu.VMEM((length, wide), F32),
            pltpu.VMEM((16, wide - n * n), F32),
            pltpu.VMEM((16, lanes), F32),
            pltpu.VMEM((wide, lanes), BF16),
            pltpu.VMEM((wide, lanes), BF16),
            pltpu.VMEM((3 * (wide - n * n), lanes), BF16),
            pltpu.VMEM((lanes, wide), BF16),
            pltpu.VMEM((lanes, wide), BF16),
            pltpu.VMEM((length, lanes), F32),
            pltpu.VMEM((nrim, length), F32),
            pltpu.VMEM((3, mn, 128), F32),
            pltpu.VMEM((peers, mn, 128), F32),
            pltpu.SemaphoreType.DMA((12 + peers,)),
            pltpu.SemaphoreType.DMA((12 + peers,)),
            pltpu.SemaphoreType.DMA((13,)),
        ] + [pltpu.VMEM(a.shape, F32) for a in args],
        compiler_params=pltpu.CompilerParams(
            collective_id=0, has_side_effects=True
        ),
    )(*args)


def solution(mesh):
    sizes = (mesh.shape["ex"], mesh.shape["ey"], mesh.shape["ez"])
    placed = (P("ez", "ey", "ex"), P(), P("ey", None, None), P(), P(), P("ey", None)) + (P(),) * 7
    return jax.shard_map(
        functools.partial(per_device, sizes), mesh=mesh, in_specs=placed,
        out_specs=P("ez", "ey", "ex"), check_vma=False,
    )
```

```python
import functools
import math

import jax
import jax.numpy as jnp
from jax import lax
from jax.experimental import pallas as pl
from jax.experimental.pallas import tpu as pltpu
from jax.sharding import PartitionSpec as P

F32 = jnp.float32
BF16 = jnp.bfloat16
I32 = jnp.int32
DIRS = ((1, 0), (-1, 0), (0, 1), (0, -1), (1, 1), (1, -1), (-1, 1), (-1, -1))


def iota(shape, dim):
    return lax.broadcasted_iota(I32, shape, dim)


def quotient(x, d):
    return (x * (65536 // d + 1)) >> 16


def onehot(mask):
    return jnp.where(mask, 1.0, 0.0).astype(F32)


def split(x):
    hi = x.astype(BF16)
    return hi, (x - hi.astype(F32)).astype(BF16)


def dg(a, b, dims):
    return lax.dot_general(a, b, ((dims[:1], dims[1:]), ((), ())), preferred_element_type=F32)


def dot3(a, b, dims=(1, 0)):
    (ah, al), (bh, bl) = a, b
    return dg(ah, bh, dims) + (dg(ah, bl, dims) + dg(al, bh, dims))


def pick(mask, values, dims=(1, 0)):
    hi, lo = split(values)
    mask = mask.astype(BF16)
    return dg(mask, hi, dims) + dg(mask, lo, dims)


def hat(index, points):
    out = jnp.zeros(index.shape, F32)
    for i in range(points):
        out = jnp.where(index == i, (1.0 - math.cos(math.pi * i / (points - 1))) / 2.0, out)
    return out


def kernel(sizes, *refs):
    inputs, out = refs[:13], refs[13]
    (
        rim, got, face, xp, xg, xr, gx, tg, gr, vv, kh, kl, k3, kth, ktl, us, back, mine, parts,
        ssem, rsem, isem,
    ) = refs[14:36]
    held = refs[36:]
    (
        res, stream, normal, span, eig_x, eig_y, eig_z,
        v_stream, v_normal, v_span, lev_x, lev_y, lev_z,
    ) = held
    nx, ny, nz = sizes
    block = stream.shape[0]
    n = block - 2
    sh = n.bit_length() - 1
    length = res.shape[2]
    ne = length // n
    main = n * n
    edge = main + 4 * n
    nrim = got.shape[0]
    rows, lanes = kh.shape
    nv, nm = v_stream.shape
    mn = nz * ny
    ix, iy, iz = lax.axis_index("ex"), lax.axis_index("ey"), lax.axis_index("ez")

    def fetch(i):
        return pltpu.make_async_copy(inputs[i], held[i], isem.at[min(i, 1)])

    for ref in (rim, got, xg, xr.at[0:16], tg.at[0:8], tg.at[length - 8 : length], gr.at[0:16]):
        ref[...] = jnp.zeros(ref.shape, F32)

    def wrap(i, size):
        return lax.rem(i + size, size)

    def where(dx, dy, dz):
        at = {}
        if dx:
            at["ex"] = wrap(ix + dx, nx)
        if dy:
            at["ey"] = iy + dy
        if dz:
            at["ez"] = wrap(iz + dz, nz)
        return at

    def has(dy):
        return jnp.logical_and(iy + dy >= 0, iy + dy < ny)

    def by_y(fn):
        fn(0)
        for dy in (1, -1):
            pl.when(has(dy))(functools.partial(fn, dy))

    barrier = pltpu.get_barrier_semaphore()

    def signal(at):
        pl.semaphore_signal(
            barrier, inc=1, device_id=at, device_id_type=pl.DeviceIdType.MESH
        )

    def greet(dy):
        for dx in (1, -1, 0):
            for dz in (1, -1, 0):
                if dx or dy or dz:
                    signal(where(dx, dy, dz))

    groups = (("ez", "ey"), ("ex",)) if mn <= 16 else (("ez",), ("ey",), ("ex",))

    def peers(axes):
        found = []
        for d in range(nz if "ez" in axes else 1):
            for f in range(ny if "ey" in axes else 1):
                for e in range(nx if "ex" in axes else 1):
                    at = {}
                    if d:
                        at["ez"] = lax.rem(iz + d, nz)
                    if f:
                        at["ey"] = lax.rem(iy + f, ny)
                    if e:
                        at["ex"] = lax.rem(ix + e, nx)
                    near = d in (0, 1, nz - 1) and e in (0, 1, nx - 1) and f < (2 if ny == 2 else 1)
                    if at:
                        found.append((at, near))
        return found

    by_y(greet)
    greeted = 8 + jnp.where(iy > 0, 9, 0) + jnp.where(iy < ny - 1, 9, 0)
    for axes in groups:
        for at, near in peers(axes):
            if not near:
                signal(at)
                greeted = greeted + 1
    for i in range(13):
        fetch(i).start()

    def shipped(src, dst, slot, at):
        return pltpu.make_async_remote_copy(
            src_ref=src, dst_ref=dst, send_sem=ssem.at[0], recv_sem=rsem.at[slot],
            device_id=at, device_id_type=pl.DeviceIdType.MESH,
        )

    def span_of(dz, dy):
        if dy == 0:
            return (0 if dz > 0 else n), n
        if dz == 0:
            return (2 * n if dy > 0 else 3 * n), n
        return 4 * n + (0 if dz > 0 else 2) + (0 if dy > 0 else 1), 1

    def halo(s):
        dz, dy = DIRS[s]
        if dy == 0:
            src = res.at[n - 1 if dz > 0 else 0]
        elif dz == 0:
            src = res.at[:, n - 1 if dy > 0 else 0]
        else:
            src = res.at[n - 1 if dz > 0 else 0, pl.ds(n - 1 if dy > 0 else 0, 1)]
        at, number = span_of(dz, dy)
        return shipped(src, rim.at[pl.ds(at, number)], 0, where(0, dy, dz))

    def ret(s):
        dz, dy = DIRS[s]
        part = pl.ds(*span_of(-dz, -dy))
        return shipped(back.at[part], got.at[part], 1, where(0, dy, dz))

    def halos(dy):
        return [halo(s) for s in range(8) if DIRS[s][1] == dy]

    def rets(dy):
        return [ret(s) for s in range(8) if DIRS[s][1] == dy]

    def planes(src, near_rows, whole, whole_rows, rest, base, dy):
        copies = []
        for dx in (1, -1):
            side = 0 if dx > 0 else 1
            near, far = near_rows[1 - side], 8 * side
            for s, (dz, sy) in enumerate(DIRS):
                if sy == dy:
                    copies.append(shipped(
                        src.at[pl.ds(near, 1), pl.ds(main, rows - main)],
                        rest.at[pl.ds(far + s, 1)], base, where(dx, dy, dz),
                    ))
            if dy == 0:
                copies.append(shipped(
                    src.at[pl.ds(near, 1), pl.ds(0, main)],
                    whole.at[pl.ds(whole_rows[side], 1), pl.ds(0, main)], base, where(dx, 0, 0),
                ))
        return copies

    def start(make):
        def go(dy):
            for c in make(dy):
                c.start()

        by_y(go)

    def take(sem, ref, count):
        bulk = ref.at[pl.ds(0, count)]
        pltpu.make_async_copy(bulk, bulk, sem).wait()

    amounts = (
        (rim, 2 * n, n + 2), (got, 2 * n, n + 2),
        (xr, 4 + 2 * main // (rows - main), 6), (gr, 4 + 2 * main // (rows - main), 6),
    )

    def settle(sem, base):
        ref, level, slope = amounts[base]
        if ny <= 2:
            take(sem, ref, level + slope * (ny - 1))
        else:
            inner = jnp.logical_and(has(1), has(-1))
            pl.when(inner)(lambda: take(sem, ref, level + 2 * slope))
            pl.when(jnp.logical_not(inner))(lambda: take(sem, ref, level + slope))

    def received(base):
        settle(rsem.at[base], base)

    def block_of(k):
        before = sum(len(peers(axes)) for axes in groups[:k])
        return before, len(peers(groups[k]))

    def begin(k):
        before, _ = block_of(k)
        for i, (at, _) in enumerate(peers(groups[k])):
            shipped(mine.at[k], parts.at[before + i], 4 + k, at).start()

    def settle_parts(sem, k):
        bulk = parts.at[pl.ds(*block_of(k))]
        pltpu.make_async_copy(bulk, bulk, sem).wait()

    def gather(k):
        before, count = block_of(k)
        settle_parts(rsem.at[4 + k], k)
        total = mine[k]
        for i in range(count):
            total = total + parts[before + i]
        return total

    hrow, hcol = iota((8, main), 0), iota((8, main), 1)
    wk, wj = hat(hcol >> sh, n), hat(hcol & (n - 1), n)
    hyz = jnp.where((hrow & 2) > 0, wk, 1.0 - wk) * jnp.where((hrow & 1) > 0, wj, 1.0 - wj)
    hyz = split(jnp.where(hrow < 4, hyz, 0.0))
    xrow, xcol = iota((length, nv), 0), iota((length, nv), 1)
    wx = hat(xrow & (n - 1), n)
    first_el = ix * ne + (xrow >> sh)
    after = jnp.where(first_el + 1 >= nv, first_el + 1 - nv, first_el + 1)
    hatx = jnp.where(xcol == first_el, 1.0 - wx, 0.0) + jnp.where(xcol == after, wx, 0.0)
    hatx = split(hatx)
    mrow, mcol = iota((mn, nz), 0), iota((mn, nz), 1)
    is_m = onehot((mrow >= mcol * ny) & (mrow < (mcol + 1) * ny))
    nrow, ncol = iota((mn, ny), 0), iota((mn, ny), 1)
    is_n = onehot(nrow - ny * quotient(nrow, ny) == ncol)
    vrow, vcol = iota((nz, 8), 0), iota((nz, 8), 1)
    vz = iz + (vcol >> 1)
    vz = jnp.where(vz >= nz, vz - nz, vz)
    at_z = onehot((vrow == vz) & (vcol < 4))
    urow, ucol = iota((ny, 8), 0), iota((ny, 8), 1)
    at_y = onehot((urow == iy + (ucol & 1)) & (ucol < 4))
    orow, ocol = iota((16, length), 0), iota((16, length), 1)
    ends = onehot(((orow == 0) & (ocol == 0)) | ((orow == 8) & (ocol == length - 1))).astype(BF16)
    face[...] = jnp.zeros_like(face)
    mine[...] = jnp.zeros_like(mine)
    vv[...] = jnp.zeros_like(vv)
    tg[8 : length - 8] = jnp.zeros((length - 16, rows), F32)

    fetch(0).wait()
    data = res[...].reshape(main, length)
    d_split = split(data)
    face[0:n] = res[n - 1]
    face[n : 2 * n] = res[0]
    face[2 * n : 3 * n] = res[:, n - 1]
    face[3 * n : 4 * n] = res[:, 0]
    for e in range(4):
        k, j = (n - 1, 0)[e >> 1], (n - 1, 0)[e & 1]
        face[4 * n + e : 4 * n + e + 1] = res[k, j : j + 1]
    xp[:, :main] = data.T
    xp[:, main:] = face[...].T
    for i in range(1, 13):
        fetch(i).wait()
    wxm = split(dot3(hatx, split(v_stream[...])))
    amat = pick(is_m, dot3(split(v_span[...].T), split(at_z)))
    amat = amat * pick(is_n, dot3(split(v_normal[...].T), split(at_y)))
    loads = dot3(split(dot3(hyz, d_split)), wxm)
    mine[0, :, :nm] = dot3(split(amat), split(loads))

    pl.semaphore_wait(barrier, greeted)
    start(lambda dy: planes(xp, (0, length - 1), xg, (0, 8), xr, 2, dy))
    start(halos)
    begin(0)

    row, col = iota((rows, block), 0), iota((rows, block), 1)
    low = row & (n - 1)
    e0 = row - edge
    rk = jnp.where(row < main, (row >> sh) + 1, low + 1)
    rk = jnp.where((row >= main) & (row < main + n), 0, rk)
    rk = jnp.where((row >= main + n) & (row < main + 2 * n), n + 1, rk)
    rk = jnp.where(row >= edge, jnp.where(e0 < 2, 0, n + 1), rk)
    rk = jnp.where(row >= edge + 4, -1, rk)
    rj = jnp.where((row >= main + 2 * n) & (row < main + 3 * n), 0, low + 1)
    rj = jnp.where((row >= main + 3 * n) & (row < main + 4 * n), n + 1, rj)
    rj = jnp.where(row >= edge, jnp.where((e0 & 1) == 0, 0, n + 1), rj)
    rj = jnp.where(row >= edge + 4, -1, rj)
    sel_k, sel_j = onehot(rk == col), onehot(rj == col)
    brow, bcol = iota((block, lanes), 0), iota((block, lanes), 1)
    bq = quotient(bcol, block)
    to_r = onehot(bq == brow)
    to_q = onehot((bcol - block * bq == brow) & (bcol < block * block))
    span_l = dot3(split(span[...]), split(to_r))
    normal_l = dot3(split(normal[...].reshape(block, block)), split(to_q))
    kmat = pick(sel_k, span_l) * pick(sel_j, normal_l)
    k_hi, k_lo = split(kmat)
    kh[...] = k_hi
    kl[...] = k_lo
    wide = rows - main
    k3[0:wide] = k_hi[main:]
    k3[wide : 2 * wide] = k_hi[main:]
    k3[2 * wide :] = k_lo[main:]
    t_hi, t_lo = split(kmat.T)
    kth[...] = t_hi
    ktl[...] = t_lo
    k_main = kh[0:main], kl[0:main]

    nep = length + 16
    pairs = ne * block
    npad = -(-pairs // 16) * 16

    def place(c):
        far = jnp.where(c == length + 8, length, -n * length)
        return jnp.where(c < length, c, jnp.where(c == length, -1, far))

    wrow, wcol = iota((npad, nep), 0), iota((npad, nep), 1)
    xi = place(wcol) + 1 - n * quotient(wrow, block)
    trow, tcol = iota((block, nep), 0), iota((block, nep), 1)
    tx = place(tcol)
    tm = (tx + 1) & (n - 1)
    s_t = split(stream[...].T)
    first = dot3(s_t, split(onehot(trow == tm)))
    second = dot3(s_t, split(onehot(trow - n == tm)))
    prow, pcol = iota((npad, block), 0), iota((npad, block), 1)
    is_p = onehot((prow - block * quotient(prow, block) == pcol) & (prow < pairs))
    wmat = jnp.where((xi >= 0) & (xi < n), pick(is_p, first), 0.0)
    wmat = wmat + jnp.where((xi >= n) & (xi < block), pick(is_p, second), 0.0)
    w_h, w_l = split(wmat[:, :length])
    w_in = jnp.concatenate([w_h, ends], axis=0), jnp.concatenate([w_l, jnp.zeros_like(ends)], axis=0)
    w_two = jnp.concatenate(w_in, axis=0)
    nin = npad + 16
    cut, tail = -(-block // 16) * 16, (pairs - block) // 16 * 16
    cols = jnp.concatenate(
        [wmat[:cut, length : length + 1], wmat[tail:, length + 8 : length + 9]], axis=0
    )
    w_back = split(wmat.T)
    eig_yz = dot3(split(jnp.broadcast_to(eig_z[...], (8, block))), split(to_r))
    eig_yz = eig_yz + dot3(split(jnp.broadcast_to(eig_y[...], (8, block))), split(to_q))
    ecol = jnp.sum(is_p * eig_x[...], axis=1, keepdims=True)
    ecol = jnp.where(iota((npad, 1), 0) < pairs, ecol, 1.0)
    inverse = 1.0 / (ecol + eig_yz[0:1])
    from_left = dot3(w_back, split(wmat[:, length : length + 1] * inverse))
    from_right = dot3(w_back, split(wmat[:, length + 8 : length + 9] * inverse))
    own_left = from_left[length : length + 1]
    own_right = from_right[length + 8 : length + 9]
    level = jnp.sum(is_m * lev_z[...], axis=1, keepdims=True)
    level = level + jnp.sum(is_n * lev_y[...], axis=1, keepdims=True) + lev_x[...]
    srow, slane = iota((8, rows - main), 0), iota((8, rows - main), 1)
    came = jnp.zeros(srow.shape, F32)
    went = jnp.zeros(srow.shape, F32)
    for s, (dz, dy) in enumerate(DIRS):
        at, number = span_of(dz, dy)
        came = jnp.where((srow == s) & (slane >= at) & (slane < at + number), 1.0, came)
        at, number = span_of(-dz, -dy)
        went = jnp.where((srow == s) & (slane >= at) & (slane < at + number), 1.0, went)
    part = dot3(split(dot3(w_in, d_split, (1, 1))), k_main)

    weights = jnp.concatenate([inverse[:cut], inverse[tail:]], axis=0) * cols
    part_ends = jnp.concatenate([part[:cut], part[tail:npad]], axis=0)
    b_two = jnp.concatenate([w_back[0][:length], w_back[1][:length]], axis=0)
    spread = split(dot3(hyz, split(amat), (0, 1)))

    received(0)
    o = dg(w_two, jnp.concatenate(split(rim[...]), axis=0), (1, 1))
    onto = o[:nin, :wide] + (o[:nin, wide:] + o[nin:, :wide])
    o_h, o_l = split(onto)
    tri = jnp.concatenate([o_h, o_l, o_h], axis=1)
    tri_ends = jnp.concatenate([tri[:cut], tri[tail:npad]], axis=0)
    modal = (part_ends + dg(tri_ends, k3[...], (1, 0))) * weights
    vv[0:1] = jnp.sum(modal[:cut], axis=0, keepdims=True)
    vv[8:9] = jnp.sum(modal[cut:], axis=0, keepdims=True)
    v_h, v_l = split(vv[...])
    o = dg(jnp.concatenate([v_h, v_l], axis=0), kth[...], (1, 0))
    gx[...] = o[:16] + (o[16:] + dg(v_h, ktl[...], (1, 0)))
    start(lambda dy: planes(gx, (0, 8), tg, (0, length - 1), gr, 3, dy))

    part = part + dg(tri, k3[...], (1, 0))
    m_h, m_l = split(part[:npad] * inverse)
    o = dg(b_two, m_h, (1, 0))
    us[...] = o[:length] + (o[length:] + dg(b_two[:length], m_l, (1, 0)))
    us[0:1] += own_right * part[npad : npad + 1]
    us[length - 1 : length] += own_left * part[npad + 8 : npad + 9]

    for k in range(len(groups) - 1):
        mine[k + 1] = gather(k)
        begin(k + 1)

    received(2)
    xg[0:1, main:] = jnp.sum(xr[0:8] * came, axis=0, keepdims=True)
    xg[8:9, main:] = jnp.sum(xr[8:16] * came, axis=0, keepdims=True)
    g_h, g_l = split(xg[...])
    o = dg(jnp.concatenate([g_h, g_l], axis=0), kh[...], (1, 0))
    hx = o[:16] + (o[16:] + dg(g_h, kl[...], (1, 0)))
    u = split(us[...] + from_left[:length] * hx[0:1] + from_right[:length] * hx[8:9])
    r_two = jnp.concatenate([kh[main : main + nrim], kl[main : main + nrim]], axis=0)
    o = dg(r_two, jnp.concatenate(u, axis=0), (1, 1))
    back[...] = o[:nrim, :length] + (o[:nrim, length:] + o[nrim:, :length])
    start(rets)
    result = dot3(k_main, u, (1, 1))

    scaled = split(gather(len(groups) - 1)[:, :nm] / level)
    coarse = dot3(scaled, wxm, (1, 1))
    result = result + dot3(spread, split(coarse))

    received(3)
    tg[0:1, main:] = jnp.sum(gr[0:8] * went, axis=0, keepdims=True)
    tg[length - 1 : length, main:] = jnp.sum(gr[8:16] * went, axis=0, keepdims=True)
    turned = tg[...].T
    out[...] = (result + turned[:main]).reshape(n, n, length)
    received(1)
    extra = got[...] + turned[main : main + nrim]
    out[n - 1] += extra[0:n]
    out[0] += extra[n : 2 * n]
    out[:, n - 1] += extra[2 * n : 3 * n]
    out[:, 0] += extra[3 * n : 4 * n]
    for e in range(4):
        k, j = (n - 1, 0)[e >> 1], (n - 1, 0)[e & 1]
        out[k, j : j + 1] += extra[4 * n + e : 4 * n + e + 1]
    for base in range(4):
        settle(ssem.at[0], base)
    for k in range(len(groups)):
        settle_parts(ssem.at[0], k)


def per_device(sizes, residual, local_stream, local_normal, local_span, eigen_stream, eigen_normal,
               eigen_span, vertex_stream, vertex_normal, vertex_span, level_stream, level_normal,
               level_span):
    nx, ny, nz = sizes
    block = local_stream.shape[0]
    n = block - 2
    length = residual.shape[2]
    nrim = 4 * n + 16
    wide = n * n + -(-nrim // 128) * 128
    lanes = -(-block * block // 128) * 128
    mn = ny * nz
    peers = mn - 1 + nx - 1 if mn <= 16 else nx + ny + nz - 3
    args = (
        residual, local_stream, local_normal.transpose(1, 0, 2), local_span,
        eigen_stream.reshape(1, -1), eigen_normal, eigen_span.reshape(1, -1), vertex_stream,
        vertex_normal, vertex_span, level_stream.reshape(1, -1), level_normal.reshape(1, -1),
        level_span.reshape(1, -1),
    )
    return pl.pallas_call(
        functools.partial(kernel, sizes),
        out_shape=pltpu.VMEM(residual.shape, F32),
        in_specs=[pl.BlockSpec(memory_space=pltpu.HBM)] * 13,
        out_specs=pl.BlockSpec(memory_space=pltpu.VMEM),
        scratch_shapes=[
            pltpu.VMEM((wide - n * n, length), F32),
            pltpu.VMEM((nrim, length), F32),
            pltpu.VMEM((wide - n * n, length), F32),
            pltpu.VMEM((length, wide), F32),
            pltpu.VMEM((16, wide), F32),
            pltpu.VMEM((24, wide - n * n), F32),
            pltpu.VMEM((16, wide), F32),
            pltpu.VMEM((length, wide), F32),
            pltpu.VMEM((24, wide - n * n), F32),
            pltpu.VMEM((16, lanes), F32),
            pltpu.VMEM((wide, lanes), BF16),
            pltpu.VMEM((wide, lanes), BF16),
            pltpu.VMEM((3 * (wide - n * n), lanes), BF16),
            pltpu.VMEM((lanes, wide), BF16),
            pltpu.VMEM((lanes, wide), BF16),
            pltpu.VMEM((length, lanes), F32),
            pltpu.VMEM((nrim, length), F32),
            pltpu.VMEM((3, mn, 128), F32),
            pltpu.VMEM((peers, mn, 128), F32),
            pltpu.SemaphoreType.DMA((1,)),
            pltpu.SemaphoreType.DMA((6 if mn <= 16 else 7,)),
            pltpu.SemaphoreType.DMA((2,)),
        ] + [pltpu.VMEM(a.shape, F32) for a in args],
        compiler_params=pltpu.CompilerParams(
            collective_id=0, has_side_effects=True
        ),
    )(*args)


def solution(mesh):
    sizes = (mesh.shape["ex"], mesh.shape["ey"], mesh.shape["ez"])
    placed = (P("ez", "ey", "ex"), P(), P("ey", None, None), P(), P(), P("ey", None)) + (P(),) * 7
    return jax.shard_map(
        functools.partial(per_device, sizes), mesh=mesh, in_specs=placed,
        out_specs=P("ez", "ey", "ex"), check_vma=False,
    )
```

```python
import functools
import math

import jax
import jax.numpy as jnp
from jax import lax
from jax.experimental import pallas as pl
from jax.experimental.pallas import tpu as pltpu
from jax.sharding import PartitionSpec as P

F32 = jnp.float32
BF16 = jnp.bfloat16
I32 = jnp.int32
DIRS = ((1, 0), (-1, 0), (0, 1), (0, -1), (1, 1), (1, -1), (-1, 1), (-1, -1))


def iota(shape, dim):
    return lax.broadcasted_iota(I32, shape, dim)


def quotient(x, d):
    return (x * (65536 // d + 1)) >> 16


def onehot(mask):
    return jnp.where(mask, 1.0, 0.0).astype(F32)


def split(x):
    hi = x.astype(BF16)
    return hi, (x - hi.astype(F32)).astype(BF16)


def dg(a, b, dims):
    return lax.dot_general(a, b, ((dims[:1], dims[1:]), ((), ())), preferred_element_type=F32)


def dot3(a, b, dims=(1, 0)):
    (ah, al), (bh, bl) = a, b
    return dg(ah, bh, dims) + (dg(ah, bl, dims) + dg(al, bh, dims))


def pick(mask, values, dims=(1, 0)):
    hi, lo = split(values)
    mask = mask.astype(BF16)
    return dg(mask, hi, dims) + dg(mask, lo, dims)


def hat(index, points):
    out = jnp.zeros(index.shape, F32)
    for i in range(points):
        out = jnp.where(index == i, (1.0 - math.cos(math.pi * i / (points - 1))) / 2.0, out)
    return out


def kernel(sizes, *refs):
    inputs, out = refs[:13], refs[13]
    (
        rim, got, face, xp, xg, xr, gx, tg, gr, vv, v0, kf, f3, kh, kl, k3, kth, ktl, us, back, mine, parts,
        ssem, rsem, isem,
    ) = refs[14:39]
    held = refs[39:]
    (
        res, stream, normal, span, eig_x, eig_y, eig_z,
        v_stream, v_normal, v_span, lev_x, lev_y, lev_z,
    ) = held
    nx, ny, nz = sizes
    block = stream.shape[0]
    n = block - 2
    sh = n.bit_length() - 1
    length = res.shape[2]
    ne = length // n
    main = n * n
    edge = main + 4 * n
    nrim = got.shape[0]
    rows, lanes = kh.shape
    nv, nm = v_stream.shape
    mn = nz * ny
    ix, iy, iz = lax.axis_index("ex"), lax.axis_index("ey"), lax.axis_index("ez")

    def fetch(i):
        return pltpu.make_async_copy(inputs[i], held[i], isem.at[min(i, 1)])

    for ref in (rim, got, xg, xr.at[0:16], tg.at[0:8], tg.at[length - 8 : length], gr.at[0:16]):
        ref[...] = jnp.zeros(ref.shape, F32)

    def wrap(i, size):
        return lax.rem(i + size, size)

    def where(dx, dy, dz):
        at = {}
        if dx:
            at["ex"] = wrap(ix + dx, nx)
        if dy:
            at["ey"] = iy + dy
        if dz:
            at["ez"] = wrap(iz + dz, nz)
        return at

    def has(dy):
        return jnp.logical_and(iy + dy >= 0, iy + dy < ny)

    def by_y(fn):
        fn(0)
        for dy in (1, -1):
            pl.when(has(dy))(functools.partial(fn, dy))

    barrier = pltpu.get_barrier_semaphore()

    def signal(at):
        pl.semaphore_signal(
            barrier, inc=1, device_id=at, device_id_type=pl.DeviceIdType.MESH
        )

    def greet(dy):
        for dx in (1, -1, 0):
            for dz in (1, -1, 0):
                if dx or dy or dz:
                    signal(where(dx, dy, dz))

    groups = (("ez", "ey"), ("ex",)) if mn <= 16 else (("ez",), ("ey",), ("ex",))

    def peers(axes):
        found = []
        for d in range(nz if "ez" in axes else 1):
            for f in range(ny if "ey" in axes else 1):
                for e in range(nx if "ex" in axes else 1):
                    at = {}
                    if d:
                        at["ez"] = lax.rem(iz + d, nz)
                    if f:
                        at["ey"] = lax.rem(iy + f, ny)
                    if e:
                        at["ex"] = lax.rem(ix + e, nx)
                    near = d in (0, 1, nz - 1) and e in (0, 1, nx - 1) and f < (2 if ny == 2 else 1)
                    if at:
                        found.append((at, near))
        return found

    by_y(greet)
    greeted = 8 + jnp.where(iy > 0, 9, 0) + jnp.where(iy < ny - 1, 9, 0)
    for axes in groups:
        for at, near in peers(axes):
            if not near:
                signal(at)
                greeted = greeted + 1
    for i in range(13):
        fetch(i).start()

    def shipped(src, dst, slot, at):
        return pltpu.make_async_remote_copy(
            src_ref=src, dst_ref=dst, send_sem=ssem.at[0], recv_sem=rsem.at[slot],
            device_id=at, device_id_type=pl.DeviceIdType.MESH,
        )

    def span_of(dz, dy):
        if dy == 0:
            return (0 if dz > 0 else n), n
        if dz == 0:
            return (2 * n if dy > 0 else 3 * n), n
        return 4 * n + (0 if dz > 0 else 2) + (0 if dy > 0 else 1), 1

    def halo(s):
        dz, dy = DIRS[s]
        if dy == 0:
            src = res.at[n - 1 if dz > 0 else 0]
        elif dz == 0:
            src = res.at[:, n - 1 if dy > 0 else 0]
        else:
            src = res.at[n - 1 if dz > 0 else 0, pl.ds(n - 1 if dy > 0 else 0, 1)]
        at, number = span_of(dz, dy)
        return shipped(src, rim.at[pl.ds(at, number)], 0, where(0, dy, dz))

    def ret(s):
        dz, dy = DIRS[s]
        part = pl.ds(*span_of(-dz, -dy))
        return shipped(back.at[part], got.at[part], 1, where(0, dy, dz))

    def halos(dy):
        return [halo(s) for s in range(8) if DIRS[s][1] == dy]

    def rets(dy):
        return [ret(s) for s in range(8) if DIRS[s][1] == dy]

    def planes(src, near_rows, whole, whole_rows, rest, base, dy):
        copies = []
        for dx in (1, -1):
            side = 0 if dx > 0 else 1
            near, far = near_rows[1 - side], 8 * side
            for s, (dz, sy) in enumerate(DIRS):
                if sy == dy:
                    copies.append(shipped(
                        src.at[pl.ds(near, 1), pl.ds(main, rows - main)],
                        rest.at[pl.ds(far + s, 1)], base, where(dx, dy, dz),
                    ))
            if dy == 0:
                copies.append(shipped(
                    src.at[pl.ds(near, 1), pl.ds(0, main)],
                    whole.at[pl.ds(whole_rows[side], 1), pl.ds(0, main)], base, where(dx, 0, 0),
                ))
        return copies

    def start(make):
        def go(dy):
            for c in make(dy):
                c.start()

        by_y(go)

    def take(sem, ref, count):
        bulk = ref.at[pl.ds(0, count)]
        pltpu.make_async_copy(bulk, bulk, sem).wait()

    amounts = (
        (rim, 2 * n, n + 2), (got, 2 * n, n + 2),
        (xr, 4 + 2 * main // (rows - main), 6), (gr, 4 + 2 * main // (rows - main), 6),
    )

    def settle(sem, base):
        ref, level, slope = amounts[base]
        if ny <= 2:
            take(sem, ref, level + slope * (ny - 1))
        else:
            inner = jnp.logical_and(has(1), has(-1))
            pl.when(inner)(lambda: take(sem, ref, level + 2 * slope))
            pl.when(jnp.logical_not(inner))(lambda: take(sem, ref, level + slope))

    def received(base):
        settle(rsem.at[base], base)

    def block_of(k):
        before = sum(len(peers(axes)) for axes in groups[:k])
        return before, len(peers(groups[k]))

    def begin(k):
        before, _ = block_of(k)
        for i, (at, _) in enumerate(peers(groups[k])):
            shipped(mine.at[k], parts.at[before + i], 4 + k, at).start()

    def settle_parts(sem, k):
        bulk = parts.at[pl.ds(*block_of(k))]
        pltpu.make_async_copy(bulk, bulk, sem).wait()

    def gather(k):
        before, count = block_of(k)
        settle_parts(rsem.at[4 + k], k)
        total = mine[k]
        for i in range(count):
            total = total + parts[before + i]
        return total

    hrow, hcol = iota((8, main), 0), iota((8, main), 1)
    wk, wj = hat(hcol >> sh, n), hat(hcol & (n - 1), n)
    hyz = jnp.where((hrow & 2) > 0, wk, 1.0 - wk) * jnp.where((hrow & 1) > 0, wj, 1.0 - wj)
    hyz = split(jnp.where(hrow < 4, hyz, 0.0))
    xrow, xcol = iota((length, nv), 0), iota((length, nv), 1)
    wx = hat(xrow & (n - 1), n)
    first_el = ix * ne + (xrow >> sh)
    after = jnp.where(first_el + 1 >= nv, first_el + 1 - nv, first_el + 1)
    hatx = jnp.where(xcol == first_el, 1.0 - wx, 0.0) + jnp.where(xcol == after, wx, 0.0)
    hatx = split(hatx)
    mrow, mcol = iota((mn, nz), 0), iota((mn, nz), 1)
    is_m = onehot((mrow >= mcol * ny) & (mrow < (mcol + 1) * ny))
    nrow, ncol = iota((mn, ny), 0), iota((mn, ny), 1)
    is_n = onehot(nrow - ny * quotient(nrow, ny) == ncol)
    vrow, vcol = iota((nz, 8), 0), iota((nz, 8), 1)
    vz = iz + (vcol >> 1)
    vz = jnp.where(vz >= nz, vz - nz, vz)
    at_z = onehot((vrow == vz) & (vcol < 4))
    urow, ucol = iota((ny, 8), 0), iota((ny, 8), 1)
    at_y = onehot((urow == iy + (ucol & 1)) & (ucol < 4))
    orow, ocol = iota((16, length), 0), iota((16, length), 1)
    ends = onehot(((orow == 0) & (ocol == 0)) | ((orow == 8) & (ocol == length - 1))).astype(BF16)
    face[...] = jnp.zeros_like(face)
    mine[...] = jnp.zeros_like(mine)
    vv[...] = jnp.zeros_like(vv)
    tg[8 : length - 8] = jnp.zeros((length - 16, rows), F32)

    fetch(0).wait()
    data = res[...].reshape(main, length)
    d_split = split(data)
    face[0:n] = res[n - 1]
    face[n : 2 * n] = res[0]
    face[2 * n : 3 * n] = res[:, n - 1]
    face[3 * n : 4 * n] = res[:, 0]
    for e in range(4):
        k, j = (n - 1, 0)[e >> 1], (n - 1, 0)[e & 1]
        face[4 * n + e : 4 * n + e + 1] = res[k, j : j + 1]
    xp[:, :main] = data.T
    xp[:, main:] = face[...].T
    for i in range(1, 13):
        fetch(i).wait()
    wxm = split(dot3(hatx, split(v_stream[...])))
    amat = pick(is_m, dot3(split(v_span[...].T), split(at_z)))
    amat = amat * pick(is_n, dot3(split(v_normal[...].T), split(at_y)))
    loads = dot3(split(dot3(hyz, d_split)), wxm)
    mine[0, :, :nm] = dot3(split(amat), split(loads))

    pl.semaphore_wait(barrier, greeted)
    start(lambda dy: planes(xp, (0, length - 1), xg, (0, 8), xr, 2, dy))
    start(halos)
    begin(0)

    row, col = iota((rows, block), 0), iota((rows, block), 1)
    low = row & (n - 1)
    e0 = row - edge
    rk = jnp.where(row < main, (row >> sh) + 1, low + 1)
    rk = jnp.where((row >= main) & (row < main + n), 0, rk)
    rk = jnp.where((row >= main + n) & (row < main + 2 * n), n + 1, rk)
    rk = jnp.where(row >= edge, jnp.where(e0 < 2, 0, n + 1), rk)
    rk = jnp.where(row >= edge + 4, -1, rk)
    rj = jnp.where((row >= main + 2 * n) & (row < main + 3 * n), 0, low + 1)
    rj = jnp.where((row >= main + 3 * n) & (row < main + 4 * n), n + 1, rj)
    rj = jnp.where(row >= edge, jnp.where((e0 & 1) == 0, 0, n + 1), rj)
    rj = jnp.where(row >= edge + 4, -1, rj)
    sel_k, sel_j = onehot(rk == col), onehot(rj == col)
    brow, bcol = iota((block, lanes), 0), iota((block, lanes), 1)
    bq = quotient(bcol, block)
    to_r = onehot(bq == brow)
    to_q = onehot((bcol - block * bq == brow) & (bcol < block * block))
    span_l = dot3(split(span[...]), split(to_r))
    normal_l = dot3(split(normal[...].reshape(block, block)), split(to_q))
    kmat = pick(sel_k, span_l) * pick(sel_j, normal_l)
    k_hi, k_lo = split(kmat)
    kh[...] = k_hi
    kl[...] = k_lo
    wide = rows - main
    kf[...] = kmat[main : main + nrim]
    k3[0:wide] = k_hi[main:]
    k3[wide : 2 * wide] = k_hi[main:]
    k3[2 * wide :] = k_lo[main:]
    t_hi, t_lo = split(kmat.T)
    kth[...] = t_hi
    ktl[...] = t_lo
    k_main = kh[0:main], kl[0:main]

    nep = length + 16
    pairs = ne * block
    npad = -(-pairs // 16) * 16

    def place(c):
        far = jnp.where(c == length + 8, length, -n * length)
        return jnp.where(c < length, c, jnp.where(c == length, -1, far))

    wrow, wcol = iota((npad, nep), 0), iota((npad, nep), 1)
    xi = place(wcol) + 1 - n * quotient(wrow, block)
    trow, tcol = iota((block, nep), 0), iota((block, nep), 1)
    tx = place(tcol)
    tm = (tx + 1) & (n - 1)
    s_t = split(stream[...].T)
    first = dot3(s_t, split(onehot(trow == tm)))
    second = dot3(s_t, split(onehot(trow - n == tm)))
    prow, pcol = iota((npad, block), 0), iota((npad, block), 1)
    is_p = onehot((prow - block * quotient(prow, block) == pcol) & (prow < pairs))
    wmat = jnp.where((xi >= 0) & (xi < n), pick(is_p, first), 0.0)
    wmat = wmat + jnp.where((xi >= n) & (xi < block), pick(is_p, second), 0.0)
    w_h, w_l = split(wmat[:, :length])
    w_in = jnp.concatenate([w_h, ends], axis=0), jnp.concatenate([w_l, jnp.zeros_like(ends)], axis=0)
    w_two = jnp.concatenate(w_in, axis=0)
    nin = npad + 16
    w_back = split(wmat.T)
    eig_yz = dot3(split(jnp.broadcast_to(eig_z[...], (8, block))), split(to_r))
    eig_yz = eig_yz + dot3(split(jnp.broadcast_to(eig_y[...], (8, block))), split(to_q))
    ecol = jnp.sum(is_p * eig_x[...], axis=1, keepdims=True)
    ecol = jnp.where(iota((npad, 1), 0) < pairs, ecol, 1.0)
    inverse = 1.0 / (ecol + eig_yz[0:1])
    from_left = dot3(w_back, split(wmat[:, length : length + 1] * inverse))
    from_right = dot3(w_back, split(wmat[:, length + 8 : length + 9] * inverse))
    own_left = from_left[length : length + 1]
    own_right = from_right[length + 8 : length + 9]
    level = jnp.sum(is_m * lev_z[...], axis=1, keepdims=True)
    level = level + jnp.sum(is_n * lev_y[...], axis=1, keepdims=True) + lev_x[...]
    srow, slane = iota((8, rows - main), 0), iota((8, rows - main), 1)
    came = jnp.zeros(srow.shape, F32)
    went = jnp.zeros(srow.shape, F32)
    for s, (dz, dy) in enumerate(DIRS):
        at, number = span_of(dz, dy)
        came = jnp.where((srow == s) & (slane >= at) & (slane < at + number), 1.0, came)
        at, number = span_of(-dz, -dy)
        went = jnp.where((srow == s) & (slane >= at) & (slane < at + number), 1.0, went)
    part = dot3(split(dot3(w_in, d_split, (1, 1))), k_main)

    for side, turn in enumerate((from_left, from_right)):
        f_h, f_l = split(turn[:length])
        for third, half in enumerate((f_h, f_h, f_l)):
            f3[third * length : (third + 1) * length, side * lanes : (side + 1) * lanes] = half
        ghost = part[:npad] * inverse * wmat[:, length + 8 * side : length + 8 * side + 1]
        v0[8 * side : 8 * side + 1] = jnp.sum(ghost, axis=0, keepdims=True)
    b_two = jnp.concatenate([w_back[0][:length], w_back[1][:length]], axis=0)
    spread = split(dot3(hyz, split(amat), (0, 1)))

    received(0)
    rim_h, rim_l = split(rim[...])
    near = jnp.concatenate([rim_h[:nrim], rim_l[:nrim], rim_h[:nrim]], axis=1)
    seen = dg(near, f3[...], (1, 0))
    for side in range(2):
        at = slice(8 * side, 8 * side + 1)
        term = seen[:, side * lanes : (side + 1) * lanes] * kf[...]
        vv[at] = v0[at] + jnp.sum(term, axis=0, keepdims=True)
    o = dg(w_two, jnp.concatenate([rim_h, rim_l], axis=0), (1, 1))
    onto = o[:nin, :wide] + (o[:nin, wide:] + o[nin:, :wide])
    o_h, o_l = split(onto)
    tri = jnp.concatenate([o_h, o_l, o_h], axis=1)
    v_h, v_l = split(vv[...])
    o = dg(jnp.concatenate([v_h, v_l], axis=0), kth[...], (1, 0))
    gx[...] = o[:16] + (o[16:] + dg(v_h, ktl[...], (1, 0)))
    start(lambda dy: planes(gx, (0, 8), tg, (0, length - 1), gr, 3, dy))

    for k in range(len(groups) - 1):
        mine[k + 1] = gather(k)
        begin(k + 1)

    received(2)
    xg[0:1, main:] = jnp.sum(xr[0:8] * came, axis=0, keepdims=True)
    xg[8:9, main:] = jnp.sum(xr[8:16] * came, axis=0, keepdims=True)
    g_h, g_l = split(xg[...])
    o = dg(jnp.concatenate([g_h, g_l], axis=0), kh[...], (1, 0))
    hx = o[:16] + (o[16:] + dg(g_h, kl[...], (1, 0)))
    part = part + dg(tri, k3[...], (1, 0))
    m_h, m_l = split(part[:npad] * inverse)
    o = dg(b_two, m_h, (1, 0))
    us[...] = o[:length] + (o[length:] + dg(b_two[:length], m_l, (1, 0)))
    us[0:1] += own_right * part[npad : npad + 1]
    us[length - 1 : length] += own_left * part[npad + 8 : npad + 9]

    u = split(us[...] + from_left[:length] * hx[0:1] + from_right[:length] * hx[8:9])
    r_two = jnp.concatenate([kh[main : main + nrim], kl[main : main + nrim]], axis=0)
    o = dg(r_two, jnp.concatenate(u, axis=0), (1, 1))
    back[...] = o[:nrim, :length] + (o[:nrim, length:] + o[nrim:, :length])
    start(rets)
    result = dot3(k_main, u, (1, 1))

    scaled = split(gather(len(groups) - 1)[:, :nm] / level)
    coarse = dot3(scaled, wxm, (1, 1))
    result = result + dot3(spread, split(coarse))

    received(3)
    tg[0:1, main:] = jnp.sum(gr[0:8] * went, axis=0, keepdims=True)
    tg[length - 1 : length, main:] = jnp.sum(gr[8:16] * went, axis=0, keepdims=True)
    turned = tg[...].T
    out[...] = (result + turned[:main]).reshape(n, n, length)
    received(1)
    extra = got[...] + turned[main : main + nrim]
    out[n - 1] += extra[0:n]
    out[0] += extra[n : 2 * n]
    out[:, n - 1] += extra[2 * n : 3 * n]
    out[:, 0] += extra[3 * n : 4 * n]
    for e in range(4):
        k, j = (n - 1, 0)[e >> 1], (n - 1, 0)[e & 1]
        out[k, j : j + 1] += extra[4 * n + e : 4 * n + e + 1]
    for base in range(4):
        settle(ssem.at[0], base)
    for k in range(len(groups)):
        settle_parts(ssem.at[0], k)


def per_device(sizes, residual, local_stream, local_normal, local_span, eigen_stream, eigen_normal,
               eigen_span, vertex_stream, vertex_normal, vertex_span, level_stream, level_normal,
               level_span):
    nx, ny, nz = sizes
    block = local_stream.shape[0]
    n = block - 2
    length = residual.shape[2]
    nrim = 4 * n + 16
    wide = n * n + -(-nrim // 128) * 128
    lanes = -(-block * block // 128) * 128
    mn = ny * nz
    peers = mn - 1 + nx - 1 if mn <= 16 else nx + ny + nz - 3
    args = (
        residual, local_stream, local_normal.transpose(1, 0, 2), local_span,
        eigen_stream.reshape(1, -1), eigen_normal, eigen_span.reshape(1, -1), vertex_stream,
        vertex_normal, vertex_span, level_stream.reshape(1, -1), level_normal.reshape(1, -1),
        level_span.reshape(1, -1),
    )
    return pl.pallas_call(
        functools.partial(kernel, sizes),
        out_shape=pltpu.VMEM(residual.shape, F32),
        in_specs=[pl.BlockSpec(memory_space=pltpu.HBM)] * 13,
        out_specs=pl.BlockSpec(memory_space=pltpu.VMEM),
        scratch_shapes=[
            pltpu.VMEM((wide - n * n, length), F32),
            pltpu.VMEM((nrim, length), F32),
            pltpu.VMEM((wide - n * n, length), F32),
            pltpu.VMEM((length, wide), F32),
            pltpu.VMEM((16, wide), F32),
            pltpu.VMEM((24, wide - n * n), F32),
            pltpu.VMEM((16, wide), F32),
            pltpu.VMEM((length, wide), F32),
            pltpu.VMEM((24, wide - n * n), F32),
            pltpu.VMEM((16, lanes), F32),
            pltpu.VMEM((16, lanes), F32),
            pltpu.VMEM((nrim, lanes), F32),
            pltpu.VMEM((3 * length, 2 * lanes), BF16),
            pltpu.VMEM((wide, lanes), BF16),
            pltpu.VMEM((wide, lanes), BF16),
            pltpu.VMEM((3 * (wide - n * n), lanes), BF16),
            pltpu.VMEM((lanes, wide), BF16),
            pltpu.VMEM((lanes, wide), BF16),
            pltpu.VMEM((length, lanes), F32),
            pltpu.VMEM((nrim, length), F32),
            pltpu.VMEM((3, mn, 128), F32),
            pltpu.VMEM((peers, mn, 128), F32),
            pltpu.SemaphoreType.DMA((1,)),
            pltpu.SemaphoreType.DMA((6 if mn <= 16 else 7,)),
            pltpu.SemaphoreType.DMA((2,)),
        ] + [pltpu.VMEM(a.shape, F32) for a in args],
        compiler_params=pltpu.CompilerParams(
            collective_id=0, has_side_effects=True
        ),
    )(*args)


def solution(mesh):
    sizes = (mesh.shape["ex"], mesh.shape["ey"], mesh.shape["ez"])
    placed = (P("ez", "ey", "ex"), P(), P("ey", None, None), P(), P(), P("ey", None)) + (P(),) * 7
    return jax.shard_map(
        functools.partial(per_device, sizes), mesh=mesh, in_specs=placed,
        out_specs=P("ez", "ey", "ex"), check_vma=False,
    )
```

```python
import functools
import math

import jax
import jax.numpy as jnp
from jax import lax
from jax.experimental import pallas as pl
from jax.experimental.pallas import tpu as pltpu
from jax.sharding import PartitionSpec as P

F32 = jnp.float32
BF16 = jnp.bfloat16
I32 = jnp.int32
DIRS = ((1, 0), (-1, 0), (0, 1), (0, -1), (1, 1), (1, -1), (-1, 1), (-1, -1))


def iota(shape, dim):
    return lax.broadcasted_iota(I32, shape, dim)


def quotient(x, d):
    return (x * (65536 // d + 1)) >> 16


def onehot(mask):
    return jnp.where(mask, 1.0, 0.0).astype(F32)


def split(x):
    hi = x.astype(BF16)
    return hi, (x - hi.astype(F32)).astype(BF16)


def dg(a, b, dims):
    return lax.dot_general(a, b, ((dims[:1], dims[1:]), ((), ())), preferred_element_type=F32)


def dot3(a, b, dims=(1, 0)):
    (ah, al), (bh, bl) = a, b
    return dg(ah, bh, dims) + (dg(ah, bl, dims) + dg(al, bh, dims))


def pick(mask, values, dims=(1, 0)):
    hi, lo = split(values)
    mask = mask.astype(BF16)
    return dg(mask, hi, dims) + dg(mask, lo, dims)


def hat(index, points):
    out = jnp.zeros(index.shape, F32)
    for i in range(points):
        out = jnp.where(index == i, (1.0 - math.cos(math.pi * i / (points - 1))) / 2.0, out)
    return out


def kernel(sizes, *refs):
    inputs, out = refs[:13], refs[13]
    (
        rim, got, face, xp, xg, xr, gx, tg, gr, vv, v0, kf, f3, kh, kl, k3, kth, ktl, us, back, mine, parts,
        ssem, rsem, isem,
    ) = refs[14:39]
    held = refs[39:]
    (
        res, stream, normal, span, eig_x, eig_y, eig_z,
        v_stream, v_normal, v_span, lev_x, lev_y, lev_z,
    ) = held
    nx, ny, nz = sizes
    block = stream.shape[0]
    n = block - 2
    sh = n.bit_length() - 1
    length = res.shape[2]
    ne = length // n
    main = n * n
    edge = main + 4 * n
    nrim = got.shape[0]
    rows, lanes = kh.shape
    nv, nm = v_stream.shape
    mn = nz * ny
    ix, iy, iz = lax.axis_index("ex"), lax.axis_index("ey"), lax.axis_index("ez")

    def fetch(i):
        return pltpu.make_async_copy(inputs[i], held[i], isem.at[min(i, 1)])

    for ref in (rim, got, xg, xr.at[0:16], tg.at[0:8], tg.at[length - 8 : length], gr.at[0:16]):
        ref[...] = jnp.zeros(ref.shape, F32)

    def wrap(i, size):
        return lax.rem(i + size, size)

    def where(dx, dy, dz):
        at = {}
        if dx:
            at["ex"] = wrap(ix + dx, nx)
        if dy:
            at["ey"] = iy + dy
        if dz:
            at["ez"] = wrap(iz + dz, nz)
        return at

    def has(dy):
        return jnp.logical_and(iy + dy >= 0, iy + dy < ny)

    def by_y(fn):
        for dy in (-1, 1):
            pl.when(has(dy))(functools.partial(fn, dy))
        fn(0)

    barrier = pltpu.get_barrier_semaphore()

    def signal(at):
        pl.semaphore_signal(
            barrier, inc=1, device_id=at, device_id_type=pl.DeviceIdType.MESH
        )

    def greet(dy):
        for dx in (1, -1, 0):
            for dz in (1, -1, 0):
                if dx or dy or dz:
                    signal(where(dx, dy, dz))

    groups = (("ez", "ey"), ("ex",)) if mn <= 16 else (("ez",), ("ey",), ("ex",))

    def peers(axes):
        found = []
        for d in range(nz if "ez" in axes else 1):
            for f in range(ny if "ey" in axes else 1):
                for e in range(nx if "ex" in axes else 1):
                    at = {}
                    if d:
                        at["ez"] = lax.rem(iz + d, nz)
                    if f:
                        at["ey"] = lax.rem(iy + f, ny)
                    if e:
                        at["ex"] = lax.rem(ix + e, nx)
                    near = d in (0, 1, nz - 1) and e in (0, 1, nx - 1) and f < (2 if ny == 2 else 1)
                    if at:
                        found.append((at, near))
        return found

    by_y(greet)
    greeted = 8 + jnp.where(iy > 0, 9, 0) + jnp.where(iy < ny - 1, 9, 0)
    for axes in groups:
        for at, near in peers(axes):
            if not near:
                signal(at)
                greeted = greeted + 1
    for i in range(13):
        fetch(i).start()

    def shipped(src, dst, slot, at):
        return pltpu.make_async_remote_copy(
            src_ref=src, dst_ref=dst, send_sem=ssem.at[0], recv_sem=rsem.at[slot],
            device_id=at, device_id_type=pl.DeviceIdType.MESH,
        )

    def span_of(dz, dy):
        if dy == 0:
            return (0 if dz > 0 else n), n
        if dz == 0:
            return (2 * n if dy > 0 else 3 * n), n
        return 4 * n + (0 if dz > 0 else 2) + (0 if dy > 0 else 1), 1

    def halo(s):
        dz, dy = DIRS[s]
        if dy == 0:
            src = res.at[n - 1 if dz > 0 else 0]
        elif dz == 0:
            src = res.at[:, n - 1 if dy > 0 else 0]
        else:
            src = res.at[n - 1 if dz > 0 else 0, pl.ds(n - 1 if dy > 0 else 0, 1)]
        at, number = span_of(dz, dy)
        return shipped(src, rim.at[pl.ds(at, number)], 0, where(0, dy, dz))

    def ret(s):
        dz, dy = DIRS[s]
        part = pl.ds(*span_of(-dz, -dy))
        return shipped(back.at[part], got.at[part], 1, where(0, dy, dz))

    def halos(dy):
        return [halo(s) for s in range(8) if DIRS[s][1] == dy]

    def rets(dy):
        return [ret(s) for s in range(8) if DIRS[s][1] == dy]

    def planes(src, near_rows, whole, whole_rows, rest, base, dy):
        copies = []
        for dx in (1, -1):
            side = 0 if dx > 0 else 1
            near, far = near_rows[1 - side], 8 * side
            for s, (dz, sy) in enumerate(DIRS):
                if sy == dy:
                    copies.append(shipped(
                        src.at[pl.ds(near, 1), pl.ds(main, rows - main)],
                        rest.at[pl.ds(far + s, 1)], base, where(dx, dy, dz),
                    ))
            if dy == 0:
                copies.append(shipped(
                    src.at[pl.ds(near, 1), pl.ds(0, main)],
                    whole.at[pl.ds(whole_rows[side], 1), pl.ds(0, main)], base, where(dx, 0, 0),
                ))
        return copies

    def start(make):
        def go(dy):
            for c in make(dy):
                c.start()

        by_y(go)

    def take(sem, ref, count):
        bulk = ref.at[pl.ds(0, count)]
        pltpu.make_async_copy(bulk, bulk, sem).wait()

    amounts = (
        (rim, 2 * n, n + 2), (got, 2 * n, n + 2),
        (xr, 4 + 2 * main // (rows - main), 6), (gr, 4 + 2 * main // (rows - main), 6),
    )

    def settle(sem, base):
        ref, level, slope = amounts[base]
        if ny <= 2:
            take(sem, ref, level + slope * (ny - 1))
        else:
            inner = jnp.logical_and(has(1), has(-1))
            pl.when(inner)(lambda: take(sem, ref, level + 2 * slope))
            pl.when(jnp.logical_not(inner))(lambda: take(sem, ref, level + slope))

    def received(base):
        settle(rsem.at[base], base)

    def block_of(k):
        before = sum(len(peers(axes)) for axes in groups[:k])
        return before, len(peers(groups[k]))

    def begin(k):
        before, _ = block_of(k)
        for i, (at, _) in enumerate(peers(groups[k])):
            shipped(mine.at[k], parts.at[before + i], 4 + k, at).start()

    def settle_parts(sem, k):
        bulk = parts.at[pl.ds(*block_of(k))]
        pltpu.make_async_copy(bulk, bulk, sem).wait()

    def gather(k):
        before, count = block_of(k)
        settle_parts(rsem.at[4 + k], k)
        total = mine[k]
        for i in range(count):
            total = total + parts[before + i]
        return total

    hrow, hcol = iota((16, main), 0), iota((16, main), 1)
    wk, wj = hat(hcol >> sh, n), hat(hcol & (n - 1), n)
    hyz = jnp.where((hrow & 2) > 0, wk, 1.0 - wk) * jnp.where((hrow & 1) > 0, wj, 1.0 - wj)
    hyz = split(jnp.where(hrow < 4, hyz, 0.0))
    hyz_two = jnp.concatenate(hyz, axis=0)
    xrow, xcol = iota((length, nv), 0), iota((length, nv), 1)
    wx = hat(xrow & (n - 1), n)
    first_el = ix * ne + (xrow >> sh)
    after = jnp.where(first_el + 1 >= nv, first_el + 1 - nv, first_el + 1)
    hatx = jnp.where(xcol == first_el, 1.0 - wx, 0.0) + jnp.where(xcol == after, wx, 0.0)
    hatx = split(hatx)
    mrow, mcol = iota((mn, nz), 0), iota((mn, nz), 1)
    is_m = onehot((mrow >= mcol * ny) & (mrow < (mcol + 1) * ny))
    nrow, ncol = iota((mn, ny), 0), iota((mn, ny), 1)
    is_n = onehot(nrow - ny * quotient(nrow, ny) == ncol)
    vrow, vcol = iota((nz, 16), 0), iota((nz, 16), 1)
    vz = iz + (vcol >> 1)
    vz = jnp.where(vz >= nz, vz - nz, vz)
    at_z = onehot((vrow == vz) & (vcol < 4))
    urow, ucol = iota((ny, 16), 0), iota((ny, 16), 1)
    at_y = onehot((urow == iy + (ucol & 1)) & (ucol < 4))
    orow, ocol = iota((16, length), 0), iota((16, length), 1)
    ends = onehot(((orow == 0) & (ocol == 0)) | ((orow == 8) & (ocol == length - 1))).astype(BF16)
    face[...] = jnp.zeros_like(face)
    mine[...] = jnp.zeros_like(mine)
    vv[...] = jnp.zeros_like(vv)
    tg[8 : length - 8] = jnp.zeros((length - 16, rows), F32)

    fetch(0).wait()
    data = res[...].reshape(main, length)
    d_split = split(data)
    face[0:n] = res[n - 1]
    face[n : 2 * n] = res[0]
    face[2 * n : 3 * n] = res[:, n - 1]
    face[3 * n : 4 * n] = res[:, 0]
    for e in range(4):
        k, j = (n - 1, 0)[e >> 1], (n - 1, 0)[e & 1]
        face[4 * n + e : 4 * n + e + 1] = res[k, j : j + 1]
    xp[:, :main] = data.T
    xp[:, main:] = face[...].T
    for i in range(1, 13):
        fetch(i).wait()
    wxm = split(dot3(hatx, split(v_stream[...])))
    amat = pick(is_m, dot3(split(v_span[...].T), split(at_z)))
    amat = amat * pick(is_n, dot3(split(v_normal[...].T), split(at_y)))
    a_h, a_l = split(amat)
    a_tri = jnp.concatenate([a_h, a_l, a_h], axis=1)
    wx_two = jnp.concatenate(wxm, axis=1)
    o = dg(hyz_two, d_split[0], (1, 0))
    o = o[:16] + (o[16:] + dg(hyz[0], d_split[1], (1, 0)))
    o = dg(jnp.concatenate(split(o), axis=0), wx_two, (1, 0))
    l_h, l_l = split(o[:16, :nm] + (o[:16, nm:] + o[16:, :nm]))
    mine[0, :, :nm] = dg(a_tri, jnp.concatenate([l_h, l_h, l_l], axis=0), (1, 0))

    pl.semaphore_wait(barrier, greeted)
    start(halos)
    start(lambda dy: planes(xp, (0, length - 1), xg, (0, 8), xr, 2, dy))
    begin(0)

    row, col = iota((rows, block), 0), iota((rows, block), 1)
    low = row & (n - 1)
    e0 = row - edge
    rk = jnp.where(row < main, (row >> sh) + 1, low + 1)
    rk = jnp.where((row >= main) & (row < main + n), 0, rk)
    rk = jnp.where((row >= main + n) & (row < main + 2 * n), n + 1, rk)
    rk = jnp.where(row >= edge, jnp.where(e0 < 2, 0, n + 1), rk)
    rk = jnp.where(row >= edge + 4, -1, rk)
    rj = jnp.where((row >= main + 2 * n) & (row < main + 3 * n), 0, low + 1)
    rj = jnp.where((row >= main + 3 * n) & (row < main + 4 * n), n + 1, rj)
    rj = jnp.where(row >= edge, jnp.where((e0 & 1) == 0, 0, n + 1), rj)
    rj = jnp.where(row >= edge + 4, -1, rj)
    sel_k, sel_j = onehot(rk == col), onehot(rj == col)
    brow, bcol = iota((block, lanes), 0), iota((block, lanes), 1)
    bq = quotient(bcol, block)
    to_r = onehot(bq == brow)
    to_q = onehot((bcol - block * bq == brow) & (bcol < block * block))
    span_l = dot3(split(span[...]), split(to_r))
    normal_l = dot3(split(normal[...].reshape(block, block)), split(to_q))
    kmat = pick(sel_k, span_l) * pick(sel_j, normal_l)
    k_hi, k_lo = split(kmat)
    kh[...] = k_hi
    kl[...] = k_lo
    wide = rows - main
    kf[...] = kmat[main : main + nrim]
    k3[0:wide] = k_hi[main:]
    k3[wide : 2 * wide] = k_hi[main:]
    k3[2 * wide :] = k_lo[main:]
    t_hi, t_lo = split(kmat.T)
    kth[...] = t_hi
    ktl[...] = t_lo
    k_main = kh[0:main], kl[0:main]

    nep = length + 16
    pairs = ne * block
    npad = -(-pairs // 16) * 16

    def place(c):
        far = jnp.where(c == length + 8, length, -n * length)
        return jnp.where(c < length, c, jnp.where(c == length, -1, far))

    wrow, wcol = iota((npad, nep), 0), iota((npad, nep), 1)
    xi = place(wcol) + 1 - n * quotient(wrow, block)
    trow, tcol = iota((block, nep), 0), iota((block, nep), 1)
    tx = place(tcol)
    tm = (tx + 1) & (n - 1)
    s_t = split(stream[...].T)
    first = dot3(s_t, split(onehot(trow == tm)))
    second = dot3(s_t, split(onehot(trow - n == tm)))
    prow, pcol = iota((npad, block), 0), iota((npad, block), 1)
    is_p = onehot((prow - block * quotient(prow, block) == pcol) & (prow < pairs))
    wmat = jnp.where((xi >= 0) & (xi < n), pick(is_p, first), 0.0)
    wmat = wmat + jnp.where((xi >= n) & (xi < block), pick(is_p, second), 0.0)
    w_h, w_l = split(wmat[:, :length])
    w_in = jnp.concatenate([w_h, ends], axis=0), jnp.concatenate([w_l, jnp.zeros_like(ends)], axis=0)
    w_two = jnp.concatenate(w_in, axis=0)
    nin = npad + 16
    w_back = split(wmat.T)
    eig_yz = dot3(split(jnp.broadcast_to(eig_z[...], (8, block))), split(to_r))
    eig_yz = eig_yz + dot3(split(jnp.broadcast_to(eig_y[...], (8, block))), split(to_q))
    ecol = jnp.sum(is_p * eig_x[...], axis=1, keepdims=True)
    ecol = jnp.where(iota((npad, 1), 0) < pairs, ecol, 1.0)
    inverse = 1.0 / (ecol + eig_yz[0:1])
    from_left = dot3(w_back, split(wmat[:, length : length + 1] * inverse))
    from_right = dot3(w_back, split(wmat[:, length + 8 : length + 9] * inverse))
    own_left = from_left[length : length + 1]
    own_right = from_right[length + 8 : length + 9]
    level = jnp.sum(is_m * lev_z[...], axis=1, keepdims=True)
    level = level + jnp.sum(is_n * lev_y[...], axis=1, keepdims=True) + lev_x[...]
    srow, slane = iota((8, rows - main), 0), iota((8, rows - main), 1)
    came = jnp.zeros(srow.shape, F32)
    went = jnp.zeros(srow.shape, F32)
    for s, (dz, dy) in enumerate(DIRS):
        at, number = span_of(dz, dy)
        came = jnp.where((srow == s) & (slane >= at) & (slane < at + number), 1.0, came)
        at, number = span_of(-dz, -dy)
        went = jnp.where((srow == s) & (slane >= at) & (slane < at + number), 1.0, went)
    part = dot3(split(dot3(w_in, d_split, (1, 1))), k_main)

    for side, turn in enumerate((from_left, from_right)):
        f_h, f_l = split(turn[:length])
        for third, half in enumerate((f_h, f_h, f_l)):
            f3[third * length : (third + 1) * length, side * lanes : (side + 1) * lanes] = half
        ghost = part[:npad] * inverse * wmat[:, length + 8 * side : length + 8 * side + 1]
        v0[8 * side : 8 * side + 1] = jnp.sum(ghost, axis=0, keepdims=True)
    b_two = jnp.concatenate([w_back[0][:length], w_back[1][:length]], axis=0)
    sp_h, sp_l = split(dot3(hyz, split(amat), (0, 1)))
    spread = jnp.concatenate([sp_h, sp_l, sp_h], axis=1)
    wx_rows = jnp.concatenate(wxm, axis=0)

    received(0)
    rim_h, rim_l = split(rim[...])
    near = jnp.concatenate([rim_h[:nrim], rim_l[:nrim], rim_h[:nrim]], axis=1)
    seen = dg(near, f3[...], (1, 0))
    for side in range(2):
        at = slice(8 * side, 8 * side + 1)
        term = seen[:, side * lanes : (side + 1) * lanes] * kf[...]
        vv[at] = v0[at] + jnp.sum(term, axis=0, keepdims=True)
    o = dg(w_two, jnp.concatenate([rim_h, rim_l], axis=0), (1, 1))
    onto = o[:nin, :wide] + (o[:nin, wide:] + o[nin:, :wide])
    o_h, o_l = split(onto)
    tri = jnp.concatenate([o_h, o_l, o_h], axis=1)
    v_h, v_l = split(vv[...])
    o = dg(jnp.concatenate([v_h, v_l], axis=0), kth[...], (1, 0))
    gx[...] = o[:16] + (o[16:] + dg(v_h, ktl[...], (1, 0)))
    start(lambda dy: planes(gx, (0, 8), tg, (0, length - 1), gr, 3, dy))

    for k in range(len(groups) - 1):
        mine[k + 1] = gather(k)
        begin(k + 1)

    received(2)
    xg[0:1, main:] = jnp.sum(xr[0:8] * came, axis=0, keepdims=True)
    xg[8:9, main:] = jnp.sum(xr[8:16] * came, axis=0, keepdims=True)
    g_h, g_l = split(xg[...])
    o = dg(jnp.concatenate([g_h, g_l], axis=0), kh[...], (1, 0))
    hx = o[:16] + (o[16:] + dg(g_h, kl[...], (1, 0)))
    part = part + dg(tri, k3[...], (1, 0))
    m_h, m_l = split(part[:npad] * inverse)
    o = dg(b_two, m_h, (1, 0))
    us[...] = o[:length] + (o[length:] + dg(b_two[:length], m_l, (1, 0)))
    us[0:1] += own_right * part[npad : npad + 1]
    us[length - 1 : length] += own_left * part[npad + 8 : npad + 9]

    u = split(us[...] + from_left[:length] * hx[0:1] + from_right[:length] * hx[8:9])
    r_two = jnp.concatenate([kh[main : main + nrim], kl[main : main + nrim]], axis=0)
    o = dg(r_two, jnp.concatenate(u, axis=0), (1, 1))
    back[...] = o[:nrim, :length] + (o[:nrim, length:] + o[nrim:, :length])
    start(rets)
    result = dot3(k_main, u, (1, 1))

    s_h, s_l = split(gather(len(groups) - 1)[:, :nm] / level)
    both = jnp.concatenate([s_h.astype(F32), s_l.astype(F32)], axis=0).astype(BF16)
    o = dg(both, wx_rows, (1, 1))
    c_h, c_l = split(o[:mn, :length] + (o[:mn, length:] + o[mn:, :length]))
    c_h = c_h.astype(F32)
    three = jnp.concatenate([c_h, c_h, c_l.astype(F32)], axis=0).astype(BF16)
    result = result + dg(spread, three, (1, 0))

    for base in range(4):
        settle(ssem.at[0], base)
    for k in range(len(groups)):
        settle_parts(ssem.at[0], k)
    received(3)
    tg[0:1, main:] = jnp.sum(gr[0:8] * went, axis=0, keepdims=True)
    tg[length - 1 : length, main:] = jnp.sum(gr[8:16] * went, axis=0, keepdims=True)
    turned = tg[...].T
    out[...] = (result + turned[:main]).reshape(n, n, length)
    received(1)
    extra = got[...] + turned[main : main + nrim]
    out[n - 1] += extra[0:n]
    out[0] += extra[n : 2 * n]
    out[:, n - 1] += extra[2 * n : 3 * n]
    out[:, 0] += extra[3 * n : 4 * n]
    for e in range(4):
        k, j = (n - 1, 0)[e >> 1], (n - 1, 0)[e & 1]
        out[k, j : j + 1] += extra[4 * n + e : 4 * n + e + 1]


def per_device(sizes, residual, local_stream, local_normal, local_span, eigen_stream, eigen_normal,
               eigen_span, vertex_stream, vertex_normal, vertex_span, level_stream, level_normal,
               level_span):
    nx, ny, nz = sizes
    block = local_stream.shape[0]
    n = block - 2
    length = residual.shape[2]
    nrim = 4 * n + 16
    wide = n * n + -(-nrim // 128) * 128
    lanes = -(-block * block // 128) * 128
    mn = ny * nz
    peers = mn - 1 + nx - 1 if mn <= 16 else nx + ny + nz - 3
    args = (
        residual, local_stream, local_normal.transpose(1, 0, 2), local_span,
        eigen_stream.reshape(1, -1), eigen_normal, eigen_span.reshape(1, -1), vertex_stream,
        vertex_normal, vertex_span, level_stream.reshape(1, -1), level_normal.reshape(1, -1),
        level_span.reshape(1, -1),
    )
    return pl.pallas_call(
        functools.partial(kernel, sizes),
        out_shape=pltpu.VMEM(residual.shape, F32),
        in_specs=[pl.BlockSpec(memory_space=pltpu.HBM)] * 13,
        out_specs=pl.BlockSpec(memory_space=pltpu.VMEM),
        scratch_shapes=[
            pltpu.VMEM((wide - n * n, length), F32),
            pltpu.VMEM((nrim, length), F32),
            pltpu.VMEM((wide - n * n, length), F32),
            pltpu.VMEM((length, wide), F32),
            pltpu.VMEM((16, wide), F32),
            pltpu.VMEM((24, wide - n * n), F32),
            pltpu.VMEM((16, wide), F32),
            pltpu.VMEM((length, wide), F32),
            pltpu.VMEM((24, wide - n * n), F32),
            pltpu.VMEM((16, lanes), F32),
            pltpu.VMEM((16, lanes), F32),
            pltpu.VMEM((nrim, lanes), F32),
            pltpu.VMEM((3 * length, 2 * lanes), BF16),
            pltpu.VMEM((wide, lanes), BF16),
            pltpu.VMEM((wide, lanes), BF16),
            pltpu.VMEM((3 * (wide - n * n), lanes), BF16),
            pltpu.VMEM((lanes, wide), BF16),
            pltpu.VMEM((lanes, wide), BF16),
            pltpu.VMEM((length, lanes), F32),
            pltpu.VMEM((nrim, length), F32),
            pltpu.VMEM((3, mn, 128), F32),
            pltpu.VMEM((peers, mn, 128), F32),
            pltpu.SemaphoreType.DMA((1,)),
            pltpu.SemaphoreType.DMA((6 if mn <= 16 else 7,)),
            pltpu.SemaphoreType.DMA((2,)),
        ] + [pltpu.VMEM(a.shape, F32) for a in args],
        compiler_params=pltpu.CompilerParams(
            collective_id=0, has_side_effects=True
        ),
    )(*args)


def solution(mesh):
    sizes = (mesh.shape["ex"], mesh.shape["ey"], mesh.shape["ez"])
    placed = (P("ez", "ey", "ex"), P(), P("ey", None, None), P(), P(), P("ey", None)) + (P(),) * 7
    return jax.shard_map(
        functools.partial(per_device, sizes), mesh=mesh, in_specs=placed,
        out_specs=P("ez", "ey", "ex"), check_vma=False,
    )
```

```python
import functools
import math

import jax
import jax.numpy as jnp
from jax import lax
from jax.experimental import pallas as pl
from jax.experimental.pallas import tpu as pltpu
from jax.sharding import PartitionSpec as P

F32 = jnp.float32
BF16 = jnp.bfloat16
I32 = jnp.int32
DIRS = ((1, 0), (-1, 0), (0, 1), (0, -1), (1, 1), (1, -1), (-1, 1), (-1, -1))


def iota(shape, dim):
    return lax.broadcasted_iota(I32, shape, dim)


def quotient(x, d):
    return (x * (65536 // d + 1)) >> 16


def onehot(mask):
    return jnp.where(mask, 1.0, 0.0).astype(F32)


def split(x):
    hi = x.astype(BF16)
    return hi, (x - hi.astype(F32)).astype(BF16)


def dg(a, b, dims):
    return lax.dot_general(a, b, ((dims[:1], dims[1:]), ((), ())), preferred_element_type=F32)


def dot3(a, b, dims=(1, 0)):
    (ah, al), (bh, bl) = a, b
    return dg(ah, bh, dims) + (dg(ah, bl, dims) + dg(al, bh, dims))


def pick(mask, values, dims=(1, 0)):
    hi, lo = split(values)
    mask = mask.astype(BF16)
    return dg(mask, hi, dims) + dg(mask, lo, dims)


def hat(index, points):
    out = jnp.zeros(index.shape, F32)
    for i in range(points):
        out = jnp.where(index == i, (1.0 - math.cos(math.pi * i / (points - 1))) / 2.0, out)
    return out


def kernel(sizes, *refs):
    inputs, out = refs[:13], refs[13]
    (
        rim, got, face, xp, xg, xr, gx, tg, gr, vv, v0, kf, f3, kh, kl, k3, kth, ktl, us, back, mine, parts,
        ssem, rsem, isem,
    ) = refs[14:39]
    held = refs[39:]
    (
        res, stream, normal, span, eig_x, eig_y, eig_z,
        v_stream, v_normal, v_span, lev_x, lev_y, lev_z,
    ) = held
    nx, ny, nz = sizes
    block = stream.shape[0]
    n = block - 2
    sh = n.bit_length() - 1
    length = res.shape[2]
    ne = length // n
    main = n * n
    edge = main + 4 * n
    nrim = got.shape[0]
    rows, lanes = kh.shape
    nv, nm = v_stream.shape
    mn = nz * ny
    ix, iy, iz = lax.axis_index("ex"), lax.axis_index("ey"), lax.axis_index("ez")

    def fetch(i):
        return pltpu.make_async_copy(inputs[i], held[i], isem.at[min(i, 1)])

    for ref in (rim, got, xg, xr.at[0:16], tg.at[0:8], tg.at[length - 8 : length], gr.at[0:16]):
        ref[...] = jnp.zeros(ref.shape, F32)

    def wrap(i, size):
        return lax.rem(i + size, size)

    def where(dx, dy, dz):
        at = {}
        if dx:
            at["ex"] = wrap(ix + dx, nx)
        if dy:
            at["ey"] = iy + dy
        if dz:
            at["ez"] = wrap(iz + dz, nz)
        return at

    def has(dy):
        return jnp.logical_and(iy + dy >= 0, iy + dy < ny)

    def by_y(fn):
        for dy in (-1, 1):
            pl.when(has(dy))(functools.partial(fn, dy))
        fn(0)

    barrier = pltpu.get_barrier_semaphore()

    def signal(at):
        pl.semaphore_signal(
            barrier, inc=1, device_id=at, device_id_type=pl.DeviceIdType.MESH
        )

    def greet(dy):
        for dx in (1, -1, 0):
            for dz in (1, -1, 0):
                if dx or dy or dz:
                    signal(where(dx, dy, dz))

    groups = (("ez", "ey"), ("ex",)) if mn <= 16 else (("ez",), ("ey",), ("ex",))

    def peers(axes):
        found = []
        for d in range(nz if "ez" in axes else 1):
            for f in range(ny if "ey" in axes else 1):
                for e in range(nx if "ex" in axes else 1):
                    at = {}
                    if d:
                        at["ez"] = lax.rem(iz + d, nz)
                    if f:
                        at["ey"] = lax.rem(iy + f, ny)
                    if e:
                        at["ex"] = lax.rem(ix + e, nx)
                    near = d in (0, 1, nz - 1) and e in (0, 1, nx - 1) and f < (2 if ny == 2 else 1)
                    if at:
                        found.append((at, near))
        return found

    fetch(0).start()
    by_y(greet)
    greeted = 8 + jnp.where(iy > 0, 9, 0) + jnp.where(iy < ny - 1, 9, 0)
    for axes in groups:
        for at, near in peers(axes):
            if not near:
                signal(at)
                greeted = greeted + 1

    for i in range(1, 13):
        fetch(i).start()

    def shipped(src, dst, slot, at):
        return pltpu.make_async_remote_copy(
            src_ref=src, dst_ref=dst, send_sem=ssem.at[0], recv_sem=rsem.at[slot],
            device_id=at, device_id_type=pl.DeviceIdType.MESH,
        )

    def span_of(dz, dy):
        if dy == 0:
            return (0 if dz > 0 else n), n
        if dz == 0:
            return (2 * n if dy > 0 else 3 * n), n
        return 4 * n + (0 if dz > 0 else 2) + (0 if dy > 0 else 1), 1

    def halo(s):
        dz, dy = DIRS[s]
        if dy == 0:
            src = res.at[n - 1 if dz > 0 else 0]
        elif dz == 0:
            src = res.at[:, n - 1 if dy > 0 else 0]
        else:
            src = res.at[n - 1 if dz > 0 else 0, pl.ds(n - 1 if dy > 0 else 0, 1)]
        at, number = span_of(dz, dy)
        return shipped(src, rim.at[pl.ds(at, number)], 0, where(0, dy, dz))

    def ret(s):
        dz, dy = DIRS[s]
        part = pl.ds(*span_of(-dz, -dy))
        return shipped(back.at[part], got.at[part], 1, where(0, dy, dz))

    def halos(dy):
        return [halo(s) for s in range(8) if DIRS[s][1] == dy]

    def rets(dy):
        return [ret(s) for s in range(8) if DIRS[s][1] == dy]

    def planes(src, near_rows, whole, whole_rows, rest, base, dy):
        copies = []
        for dx in (1, -1):
            side = 0 if dx > 0 else 1
            near, far = near_rows[1 - side], 8 * side
            for s, (dz, sy) in enumerate(DIRS):
                if sy == dy:
                    copies.append(shipped(
                        src.at[pl.ds(near, 1), pl.ds(main, rows - main)],
                        rest.at[pl.ds(far + s, 1)], base, where(dx, dy, dz),
                    ))
            if dy == 0:
                copies.append(shipped(
                    src.at[pl.ds(near, 1), pl.ds(0, main)],
                    whole.at[pl.ds(whole_rows[side], 1), pl.ds(0, main)], base, where(dx, 0, 0),
                ))
        return copies

    def start(make):
        def go(dy):
            for c in make(dy):
                c.start()

        by_y(go)

    def take(sem, ref, count):
        bulk = ref.at[pl.ds(0, count)]
        pltpu.make_async_copy(bulk, bulk, sem).wait()

    amounts = (
        (rim, 2 * n, n + 2), (got, 2 * n, n + 2),
        (xr, 4 + 2 * main // (rows - main), 6), (gr, 4 + 2 * main // (rows - main), 6),
    )

    def settle(sem, base):
        ref, level, slope = amounts[base]
        if ny <= 2:
            take(sem, ref, level + slope * (ny - 1))
        else:
            inner = jnp.logical_and(has(1), has(-1))
            pl.when(inner)(lambda: take(sem, ref, level + 2 * slope))
            pl.when(jnp.logical_not(inner))(lambda: take(sem, ref, level + slope))

    def received(base):
        settle(rsem.at[base], base)

    def block_of(k):
        before = sum(len(peers(axes)) for axes in groups[:k])
        return before, len(peers(groups[k]))

    def begin(k):
        before, _ = block_of(k)
        for i, (at, _) in enumerate(peers(groups[k])):
            shipped(mine.at[k], parts.at[before + i], 4 + k, at).start()

    def settle_parts(sem, k):
        bulk = parts.at[pl.ds(*block_of(k))]
        pltpu.make_async_copy(bulk, bulk, sem).wait()

    def gather(k):
        before, count = block_of(k)
        settle_parts(rsem.at[4 + k], k)
        total = mine[k]
        for i in range(count):
            total = total + parts[before + i]
        return total

    hrow, hcol = iota((16, main), 0), iota((16, main), 1)
    wk, wj = hat(hcol >> sh, n), hat(hcol & (n - 1), n)
    hyz = jnp.where((hrow & 2) > 0, wk, 1.0 - wk) * jnp.where((hrow & 1) > 0, wj, 1.0 - wj)
    hyz = split(jnp.where(hrow < 4, hyz, 0.0))
    hyz_two = jnp.concatenate(hyz, axis=0)
    xrow, xcol = iota((length, nv), 0), iota((length, nv), 1)
    wx = hat(xrow & (n - 1), n)
    first_el = ix * ne + (xrow >> sh)
    after = jnp.where(first_el + 1 >= nv, first_el + 1 - nv, first_el + 1)
    hatx = jnp.where(xcol == first_el, 1.0 - wx, 0.0) + jnp.where(xcol == after, wx, 0.0)
    hatx = split(hatx)
    mrow, mcol = iota((mn, nz), 0), iota((mn, nz), 1)
    is_m = onehot((mrow >= mcol * ny) & (mrow < (mcol + 1) * ny))
    nrow, ncol = iota((mn, ny), 0), iota((mn, ny), 1)
    is_n = onehot(nrow - ny * quotient(nrow, ny) == ncol)
    vrow, vcol = iota((nz, 16), 0), iota((nz, 16), 1)
    vz = iz + (vcol >> 1)
    vz = jnp.where(vz >= nz, vz - nz, vz)
    at_z = onehot((vrow == vz) & (vcol < 4))
    urow, ucol = iota((ny, 16), 0), iota((ny, 16), 1)
    at_y = onehot((urow == iy + (ucol & 1)) & (ucol < 4))
    orow, ocol = iota((16, length), 0), iota((16, length), 1)
    ends = onehot(((orow == 0) & (ocol == 0)) | ((orow == 8) & (ocol == length - 1))).astype(BF16)
    face[...] = jnp.zeros_like(face)
    mine[...] = jnp.zeros_like(mine)
    vv[...] = jnp.zeros_like(vv)
    tg[8 : length - 8] = jnp.zeros((length - 16, rows), F32)

    fetch(0).wait()
    data = res[...].reshape(main, length)
    d_split = split(data)
    face[0:n] = res[n - 1]
    face[n : 2 * n] = res[0]
    face[2 * n : 3 * n] = res[:, n - 1]
    face[3 * n : 4 * n] = res[:, 0]
    for e in range(4):
        k, j = (n - 1, 0)[e >> 1], (n - 1, 0)[e & 1]
        face[4 * n + e : 4 * n + e + 1] = res[k, j : j + 1]
    xp[:, :main] = data.T
    xp[:, main:] = face[...].T
    for i in range(1, 13):
        fetch(i).wait()
    wxm = split(dot3(hatx, split(v_stream[...])))
    amat = pick(is_m, dot3(split(v_span[...].T), split(at_z)))
    amat = amat * pick(is_n, dot3(split(v_normal[...].T), split(at_y)))
    a_h, a_l = split(amat)
    a_tri = jnp.concatenate([a_h, a_l, a_h], axis=1)
    wx_two = jnp.concatenate(wxm, axis=1)
    o = dg(hyz_two, d_split[0], (1, 0))
    o = o[:16] + (o[16:] + dg(hyz[0], d_split[1], (1, 0)))
    o = dg(jnp.concatenate(split(o), axis=0), wx_two, (1, 0))
    l_h, l_l = split(o[:16, :nm] + (o[:16, nm:] + o[16:, :nm]))
    mine[0, :, :nm] = dg(a_tri, jnp.concatenate([l_h, l_h, l_l], axis=0), (1, 0))

    pl.semaphore_wait(barrier, greeted)
    start(halos)
    start(lambda dy: planes(xp, (0, length - 1), xg, (0, 8), xr, 2, dy))
    begin(0)

    row, col = iota((rows, block), 0), iota((rows, block), 1)
    low = row & (n - 1)
    e0 = row - edge
    rk = jnp.where(row < main, (row >> sh) + 1, low + 1)
    rk = jnp.where((row >= main) & (row < main + n), 0, rk)
    rk = jnp.where((row >= main + n) & (row < main + 2 * n), n + 1, rk)
    rk = jnp.where(row >= edge, jnp.where(e0 < 2, 0, n + 1), rk)
    rk = jnp.where(row >= edge + 4, -1, rk)
    rj = jnp.where((row >= main + 2 * n) & (row < main + 3 * n), 0, low + 1)
    rj = jnp.where((row >= main + 3 * n) & (row < main + 4 * n), n + 1, rj)
    rj = jnp.where(row >= edge, jnp.where((e0 & 1) == 0, 0, n + 1), rj)
    rj = jnp.where(row >= edge + 4, -1, rj)
    sel_k, sel_j = onehot(rk == col), onehot(rj == col)
    brow, bcol = iota((block, lanes), 0), iota((block, lanes), 1)
    bq = quotient(bcol, block)
    to_r = onehot(bq == brow)
    to_q = onehot((bcol - block * bq == brow) & (bcol < block * block))
    span_l = dot3(split(span[...]), split(to_r))
    normal_l = dot3(split(normal[...].reshape(block, block)), split(to_q))
    kmat = pick(sel_k, span_l) * pick(sel_j, normal_l)
    k_hi, k_lo = split(kmat)
    kh[...] = k_hi
    kl[...] = k_lo
    wide = rows - main
    kf[...] = kmat[main : main + nrim]
    k3[0:wide] = k_hi[main:]
    k3[wide : 2 * wide] = k_hi[main:]
    k3[2 * wide :] = k_lo[main:]
    t_hi, t_lo = split(kmat.T)
    kth[...] = t_hi
    ktl[...] = t_lo
    k_main = kh[0:main], kl[0:main]

    nep = length + 16
    pairs = ne * block
    npad = -(-pairs // 16) * 16

    def place(c):
        far = jnp.where(c == length + 8, length, -n * length)
        return jnp.where(c < length, c, jnp.where(c == length, -1, far))

    wrow, wcol = iota((npad, nep), 0), iota((npad, nep), 1)
    xi = place(wcol) + 1 - n * quotient(wrow, block)
    trow, tcol = iota((block, nep), 0), iota((block, nep), 1)
    tx = place(tcol)
    tm = (tx + 1) & (n - 1)
    s_t = split(stream[...].T)
    first = dot3(s_t, split(onehot(trow == tm)))
    second = dot3(s_t, split(onehot(trow - n == tm)))
    prow, pcol = iota((npad, block), 0), iota((npad, block), 1)
    is_p = onehot((prow - block * quotient(prow, block) == pcol) & (prow < pairs))
    wmat = jnp.where((xi >= 0) & (xi < n), pick(is_p, first), 0.0)
    wmat = wmat + jnp.where((xi >= n) & (xi < block), pick(is_p, second), 0.0)
    w_h, w_l = split(wmat[:, :length])
    w_in = jnp.concatenate([w_h, ends], axis=0), jnp.concatenate([w_l, jnp.zeros_like(ends)], axis=0)
    w_two = jnp.concatenate(w_in, axis=0)
    nin = npad + 16
    w_back = split(wmat.T)
    eig_yz = dot3(split(jnp.broadcast_to(eig_z[...], (8, block))), split(to_r))
    eig_yz = eig_yz + dot3(split(jnp.broadcast_to(eig_y[...], (8, block))), split(to_q))
    ecol = jnp.sum(is_p * eig_x[...], axis=1, keepdims=True)
    ecol = jnp.where(iota((npad, 1), 0) < pairs, ecol, 1.0)
    inverse = 1.0 / (ecol + eig_yz[0:1])
    from_left = dot3(w_back, split(wmat[:, length : length + 1] * inverse))
    from_right = dot3(w_back, split(wmat[:, length + 8 : length + 9] * inverse))
    own_left = from_left[length : length + 1]
    own_right = from_right[length + 8 : length + 9]
    level = jnp.sum(is_m * lev_z[...], axis=1, keepdims=True)
    level = level + jnp.sum(is_n * lev_y[...], axis=1, keepdims=True) + lev_x[...]
    srow, slane = iota((8, rows - main), 0), iota((8, rows - main), 1)
    came = jnp.zeros(srow.shape, F32)
    went = jnp.zeros(srow.shape, F32)
    for s, (dz, dy) in enumerate(DIRS):
        at, number = span_of(dz, dy)
        came = jnp.where((srow == s) & (slane >= at) & (slane < at + number), 1.0, came)
        at, number = span_of(-dz, -dy)
        went = jnp.where((srow == s) & (slane >= at) & (slane < at + number), 1.0, went)
    part = dot3(split(dot3(w_in, d_split, (1, 1))), k_main)

    for side, turn in enumerate((from_left, from_right)):
        f_h, f_l = split(turn[:length])
        for third, half in enumerate((f_h, f_h, f_l)):
            f3[third * length : (third + 1) * length, side * lanes : (side + 1) * lanes] = half
        ghost = part[:npad] * inverse * wmat[:, length + 8 * side : length + 8 * side + 1]
        v0[8 * side : 8 * side + 1] = jnp.sum(ghost, axis=0, keepdims=True)
    b_two = jnp.concatenate([w_back[0][:length], w_back[1][:length]], axis=0)
    sp_h, sp_l = split(dot3(hyz, split(amat), (0, 1)))
    spread = jnp.concatenate([sp_h, sp_l, sp_h], axis=1)
    wx_rows = jnp.concatenate(wxm, axis=0)

    received(0)
    rim_h, rim_l = split(rim[...])
    near = jnp.concatenate([rim_h[:nrim], rim_l[:nrim], rim_h[:nrim]], axis=1)
    seen = dg(near, f3[...], (1, 0))
    for side in range(2):
        at = slice(8 * side, 8 * side + 1)
        term = seen[:, side * lanes : (side + 1) * lanes] * kf[...]
        vv[at] = v0[at] + jnp.sum(term, axis=0, keepdims=True)
    o = dg(w_two, jnp.concatenate([rim_h, rim_l], axis=0), (1, 1))
    onto = o[:nin, :wide] + (o[:nin, wide:] + o[nin:, :wide])
    o_h, o_l = split(onto)
    tri = jnp.concatenate([o_h, o_l, o_h], axis=1)
    v_h, v_l = split(vv[...])
    o = dg(jnp.concatenate([v_h, v_l], axis=0), kth[...], (1, 0))
    gx[...] = o[:16] + (o[16:] + dg(v_h, ktl[...], (1, 0)))
    start(lambda dy: planes(gx, (0, 8), tg, (0, length - 1), gr, 3, dy))

    for k in range(len(groups) - 1):
        mine[k + 1] = gather(k)
        begin(k + 1)

    received(2)
    xg[0:1, main:] = jnp.sum(xr[0:8] * came, axis=0, keepdims=True)
    xg[8:9, main:] = jnp.sum(xr[8:16] * came, axis=0, keepdims=True)
    g_h, g_l = split(xg[...])
    o = dg(jnp.concatenate([g_h, g_l], axis=0), kh[...], (1, 0))
    hx = o[:16] + (o[16:] + dg(g_h, kl[...], (1, 0)))
    part = part + dg(tri, k3[...], (1, 0))
    m_h, m_l = split(part[:npad] * inverse)
    o = dg(b_two, m_h, (1, 0))
    us[...] = o[:length] + (o[length:] + dg(b_two[:length], m_l, (1, 0)))
    us[0:1] += own_right * part[npad : npad + 1]
    us[length - 1 : length] += own_left * part[npad + 8 : npad + 9]

    u = split(us[...] + from_left[:length] * hx[0:1] + from_right[:length] * hx[8:9])
    r_two = jnp.concatenate([kh[main : main + nrim], kl[main : main + nrim]], axis=0)
    o = dg(r_two, jnp.concatenate(u, axis=0), (1, 1))
    back[...] = o[:nrim, :length] + (o[:nrim, length:] + o[nrim:, :length])
    start(rets)
    result = dot3(k_main, u, (1, 1))

    s_h, s_l = split(gather(len(groups) - 1)[:, :nm] / level)
    both = jnp.concatenate([s_h.astype(F32), s_l.astype(F32)], axis=0).astype(BF16)
    o = dg(both, wx_rows, (1, 1))
    c_h, c_l = split(o[:mn, :length] + (o[:mn, length:] + o[mn:, :length]))
    c_h = c_h.astype(F32)
    three = jnp.concatenate([c_h, c_h, c_l.astype(F32)], axis=0).astype(BF16)
    result = result + dg(spread, three, (1, 0))

    for base in range(4):
        settle(ssem.at[0], base)
    for k in range(len(groups)):
        settle_parts(ssem.at[0], k)
    received(3)
    tg[0:1, main:] = jnp.sum(gr[0:8] * went, axis=0, keepdims=True)
    tg[length - 1 : length, main:] = jnp.sum(gr[8:16] * went, axis=0, keepdims=True)
    turned = tg[...].T
    out[...] = (result + turned[:main]).reshape(n, n, length)
    received(1)
    extra = got[...] + turned[main : main + nrim]
    out[n - 1] += extra[0:n]
    out[0] += extra[n : 2 * n]
    out[:, n - 1] += extra[2 * n : 3 * n]
    out[:, 0] += extra[3 * n : 4 * n]
    for e in range(4):
        k, j = (n - 1, 0)[e >> 1], (n - 1, 0)[e & 1]
        out[k, j : j + 1] += extra[4 * n + e : 4 * n + e + 1]


def per_device(sizes, residual, local_stream, local_normal, local_span, eigen_stream, eigen_normal,
               eigen_span, vertex_stream, vertex_normal, vertex_span, level_stream, level_normal,
               level_span):
    nx, ny, nz = sizes
    block = local_stream.shape[0]
    n = block - 2
    length = residual.shape[2]
    nrim = 4 * n + 16
    wide = n * n + -(-nrim // 128) * 128
    lanes = -(-block * block // 128) * 128
    mn = ny * nz
    peers = mn - 1 + nx - 1 if mn <= 16 else nx + ny + nz - 3
    args = (
        residual, local_stream, local_normal.transpose(1, 0, 2), local_span,
        eigen_stream.reshape(1, -1), eigen_normal, eigen_span.reshape(1, -1), vertex_stream,
        vertex_normal, vertex_span, level_stream.reshape(1, -1), level_normal.reshape(1, -1),
        level_span.reshape(1, -1),
    )
    return pl.pallas_call(
        functools.partial(kernel, sizes),
        out_shape=pltpu.VMEM(residual.shape, F32),
        in_specs=[pl.BlockSpec(memory_space=pltpu.HBM)] * 13,
        out_specs=pl.BlockSpec(memory_space=pltpu.VMEM),
        scratch_shapes=[
            pltpu.VMEM((wide - n * n, length), F32),
            pltpu.VMEM((nrim, length), F32),
            pltpu.VMEM((wide - n * n, length), F32),
            pltpu.VMEM((length, wide), F32),
            pltpu.VMEM((16, wide), F32),
            pltpu.VMEM((24, wide - n * n), F32),
            pltpu.VMEM((16, wide), F32),
            pltpu.VMEM((length, wide), F32),
            pltpu.VMEM((24, wide - n * n), F32),
            pltpu.VMEM((16, lanes), F32),
            pltpu.VMEM((16, lanes), F32),
            pltpu.VMEM((nrim, lanes), F32),
            pltpu.VMEM((3 * length, 2 * lanes), BF16),
            pltpu.VMEM((wide, lanes), BF16),
            pltpu.VMEM((wide, lanes), BF16),
            pltpu.VMEM((3 * (wide - n * n), lanes), BF16),
            pltpu.VMEM((lanes, wide), BF16),
            pltpu.VMEM((lanes, wide), BF16),
            pltpu.VMEM((length, lanes), F32),
            pltpu.VMEM((nrim, length), F32),
            pltpu.VMEM((3, mn, vertex_stream.shape[1]), F32),
            pltpu.VMEM((peers, mn, vertex_stream.shape[1]), F32),
            pltpu.SemaphoreType.DMA((1,)),
            pltpu.SemaphoreType.DMA((6 if mn <= 16 else 7,)),
            pltpu.SemaphoreType.DMA((2,)),
        ] + [pltpu.VMEM(a.shape, F32) for a in args],
        compiler_params=pltpu.CompilerParams(
            collective_id=0, has_side_effects=True
        ),
    )(*args)


def solution(mesh):
    sizes = (mesh.shape["ex"], mesh.shape["ey"], mesh.shape["ez"])
    placed = (P("ez", "ey", "ex"), P(), P("ey", None, None), P(), P(), P("ey", None)) + (P(),) * 7
    return jax.shard_map(
        functools.partial(per_device, sizes), mesh=mesh, in_specs=placed,
        out_specs=P("ez", "ey", "ex"), check_vma=False,
    )
```

```python
import functools
import math

import jax
import jax.numpy as jnp
from jax import lax
from jax.experimental import pallas as pl
from jax.experimental.pallas import tpu as pltpu
from jax.sharding import PartitionSpec as P

F32 = jnp.float32
BF16 = jnp.bfloat16
I32 = jnp.int32
DIRS = ((1, 0), (-1, 0), (0, 1), (0, -1), (1, 1), (1, -1), (-1, 1), (-1, -1))


def iota(shape, dim):
    return lax.broadcasted_iota(I32, shape, dim)


def quotient(x, d):
    return (x * (65536 // d + 1)) >> 16


def onehot(mask):
    return jnp.where(mask, 1.0, 0.0).astype(F32)


def split(x):
    hi = x.astype(BF16)
    return hi, (x - hi.astype(F32)).astype(BF16)


def dg(a, b, dims):
    return lax.dot_general(a, b, ((dims[:1], dims[1:]), ((), ())), preferred_element_type=F32)


def dot3(a, b, dims=(1, 0)):
    (ah, al), (bh, bl) = a, b
    return dg(ah, bh, dims) + (dg(ah, bl, dims) + dg(al, bh, dims))


def pick(mask, values, dims=(1, 0)):
    hi, lo = split(values)
    mask = mask.astype(BF16)
    return dg(mask, hi, dims) + dg(mask, lo, dims)


def hat(index, points):
    out = jnp.zeros(index.shape, F32)
    for i in range(points):
        out = jnp.where(index == i, (1.0 - math.cos(math.pi * i / (points - 1))) / 2.0, out)
    return out


def kernel(sizes, *refs):
    inputs, out = refs[:13], refs[13]
    (
        rim, got, face, xp, xg, xr, gx, tg, gr, vv, v0, kf, f3, kh, kl, k3, kth, ktl, us, back, mine, parts,
        ssem, rsem,
    ) = refs[14:38]
    held = refs[38:]
    (
        res, stream, normal, span, eig_x, eig_y, eig_z,
        v_stream, v_normal, v_span, lev_x, lev_y, lev_z,
    ) = held
    nx, ny, nz = sizes
    block = stream.shape[0]
    n = block - 2
    sh = n.bit_length() - 1
    length = res.shape[2]
    ne = length // n
    main = n * n
    edge = main + 4 * n
    nrim = got.shape[0]
    rows, lanes = kh.shape
    nv, nm = v_stream.shape
    mn = nz * ny
    ix, iy, iz = lax.axis_index("ex"), lax.axis_index("ey"), lax.axis_index("ez")

    def fetch(i):
        return pltpu.make_async_copy(inputs[i], held[i], ssem.at[0] if i else rsem.at[1])

    for ref in (rim, got, xg, xr.at[0:16], tg.at[0:8], tg.at[length - 8 : length], gr.at[0:16]):
        ref[...] = jnp.zeros(ref.shape, F32)

    def wrap(i, size):
        return lax.rem(i + size, size)

    def where(dx, dy, dz):
        at = {}
        if dx:
            at["ex"] = wrap(ix + dx, nx)
        if dy:
            at["ey"] = iy + dy
        if dz:
            at["ez"] = wrap(iz + dz, nz)
        return at

    def has(dy):
        return jnp.logical_and(iy + dy >= 0, iy + dy < ny)

    def by_y(fn):
        for dy in (-1, 1):
            pl.when(has(dy))(functools.partial(fn, dy))
        fn(0)

    barrier = pltpu.get_barrier_semaphore()

    def signal(at):
        pl.semaphore_signal(
            barrier, inc=1, device_id=at, device_id_type=pl.DeviceIdType.MESH
        )

    def greet(dy):
        for dx in (1, -1, 0):
            for dz in (1, -1, 0):
                if dx or dy or dz:
                    signal(where(dx, dy, dz))

    groups = (("ez", "ey"), ("ex",)) if mn <= 16 else (("ez",), ("ey",), ("ex",))

    def peers(axes):
        found = []
        for d in range(nz if "ez" in axes else 1):
            for f in range(ny if "ey" in axes else 1):
                for e in range(nx if "ex" in axes else 1):
                    at = {}
                    if d:
                        at["ez"] = lax.rem(iz + d, nz)
                    if f:
                        at["ey"] = lax.rem(iy + f, ny)
                    if e:
                        at["ex"] = lax.rem(ix + e, nx)
                    near = d in (0, 1, nz - 1) and e in (0, 1, nx - 1) and f < (2 if ny == 2 else 1)
                    if at:
                        found.append((at, near))
        return found

    fetch(0).start()
    by_y(greet)
    greeted = 8 + jnp.where(iy > 0, 9, 0) + jnp.where(iy < ny - 1, 9, 0)
    for axes in groups:
        for at, near in peers(axes):
            if not near:
                signal(at)
                greeted = greeted + 1

    for i in range(1, 13):
        fetch(i).start()

    def shipped(src, dst, slot, at):
        return pltpu.make_async_remote_copy(
            src_ref=src, dst_ref=dst, send_sem=ssem.at[0], recv_sem=rsem.at[slot],
            device_id=at, device_id_type=pl.DeviceIdType.MESH,
        )

    def span_of(dz, dy):
        if dy == 0:
            return (0 if dz > 0 else n), n
        if dz == 0:
            return (2 * n if dy > 0 else 3 * n), n
        return 4 * n + (0 if dz > 0 else 2) + (0 if dy > 0 else 1), 1

    def halo(s):
        dz, dy = DIRS[s]
        if dy == 0:
            src = res.at[n - 1 if dz > 0 else 0]
        elif dz == 0:
            src = res.at[:, n - 1 if dy > 0 else 0]
        else:
            src = res.at[n - 1 if dz > 0 else 0, pl.ds(n - 1 if dy > 0 else 0, 1)]
        at, number = span_of(dz, dy)
        return shipped(src, rim.at[pl.ds(at, number)], 0, where(0, dy, dz))

    def ret(s):
        dz, dy = DIRS[s]
        part = pl.ds(*span_of(-dz, -dy))
        return shipped(back.at[part], got.at[part], 1, where(0, dy, dz))

    def halos(dy):
        return [halo(s) for s in range(8) if DIRS[s][1] == dy]

    def rets(dy):
        return [ret(s) for s in range(8) if DIRS[s][1] == dy]

    def planes(src, near_rows, whole, whole_rows, rest, base, dy):
        copies = []
        for dx in (1, -1):
            side = 0 if dx > 0 else 1
            near, far = near_rows[1 - side], 8 * side
            for s, (dz, sy) in enumerate(DIRS):
                if sy == dy:
                    copies.append(shipped(
                        src.at[pl.ds(near, 1), pl.ds(main, rows - main)],
                        rest.at[pl.ds(far + s, 1)], base, where(dx, dy, dz),
                    ))
            if dy == 0:
                copies.append(shipped(
                    src.at[pl.ds(near, 1), pl.ds(0, main)],
                    whole.at[pl.ds(whole_rows[side], 1), pl.ds(0, main)], base, where(dx, 0, 0),
                ))
        return copies

    def start(make):
        def go(dy):
            for c in make(dy):
                c.start()

        by_y(go)

    def take(sem, ref, count):
        bulk = ref.at[pl.ds(0, count)]
        pltpu.make_async_copy(bulk, bulk, sem).wait()

    amounts = (
        (rim, 2 * n, n + 2), (got, 2 * n, n + 2),
        (xr, 4 + 2 * main // (rows - main), 6), (gr, 4 + 2 * main // (rows - main), 6),
    )

    def settle(sem, base):
        ref, level, slope = amounts[base]
        if ny <= 2:
            take(sem, ref, level + slope * (ny - 1))
        else:
            inner = jnp.logical_and(has(1), has(-1))
            pl.when(inner)(lambda: take(sem, ref, level + 2 * slope))
            pl.when(jnp.logical_not(inner))(lambda: take(sem, ref, level + slope))

    def received(base):
        settle(rsem.at[base], base)

    def block_of(k):
        before = sum(len(peers(axes)) for axes in groups[:k])
        return before, len(peers(groups[k]))

    def begin(k):
        before, _ = block_of(k)
        for i, (at, _) in enumerate(peers(groups[k])):
            shipped(mine.at[k], parts.at[before + i], 4 + k, at).start()

    def settle_parts(sem, k):
        bulk = parts.at[pl.ds(*block_of(k))]
        pltpu.make_async_copy(bulk, bulk, sem).wait()

    def gather(k):
        before, count = block_of(k)
        settle_parts(rsem.at[4 + k], k)
        total = mine[k]
        for i in range(count):
            total = total + parts[before + i]
        return total

    hrow, hcol = iota((16, main), 0), iota((16, main), 1)
    wk, wj = hat(hcol >> sh, n), hat(hcol & (n - 1), n)
    hyz = jnp.where((hrow & 2) > 0, wk, 1.0 - wk) * jnp.where((hrow & 1) > 0, wj, 1.0 - wj)
    hyz = split(jnp.where(hrow < 4, hyz, 0.0))
    hyz_two = jnp.concatenate(hyz, axis=0)
    xrow, xcol = iota((length, nv), 0), iota((length, nv), 1)
    wx = hat(xrow & (n - 1), n)
    first_el = ix * ne + (xrow >> sh)
    after = jnp.where(first_el + 1 >= nv, first_el + 1 - nv, first_el + 1)
    hatx = jnp.where(xcol == first_el, 1.0 - wx, 0.0) + jnp.where(xcol == after, wx, 0.0)
    hatx = split(hatx)
    mrow, mcol = iota((mn, nz), 0), iota((mn, nz), 1)
    is_m = onehot((mrow >= mcol * ny) & (mrow < (mcol + 1) * ny))
    nrow, ncol = iota((mn, ny), 0), iota((mn, ny), 1)
    is_n = onehot(nrow - ny * quotient(nrow, ny) == ncol)
    vrow, vcol = iota((nz, 16), 0), iota((nz, 16), 1)
    vz = iz + (vcol >> 1)
    vz = jnp.where(vz >= nz, vz - nz, vz)
    at_z = onehot((vrow == vz) & (vcol < 4))
    urow, ucol = iota((ny, 16), 0), iota((ny, 16), 1)
    at_y = onehot((urow == iy + (ucol & 1)) & (ucol < 4))
    orow, ocol = iota((16, length), 0), iota((16, length), 1)
    ends = onehot(((orow == 0) & (ocol == 0)) | ((orow == 8) & (ocol == length - 1))).astype(BF16)
    face[...] = jnp.zeros_like(face)
    mine[...] = jnp.zeros_like(mine)
    vv[...] = jnp.zeros_like(vv)
    tg[8 : length - 8] = jnp.zeros((length - 16, rows), F32)

    fetch(0).wait()
    data = res[...].reshape(main, length)
    d_split = split(data)
    face[0:n] = res[n - 1]
    face[n : 2 * n] = res[0]
    face[2 * n : 3 * n] = res[:, n - 1]
    face[3 * n : 4 * n] = res[:, 0]
    for e in range(4):
        k, j = (n - 1, 0)[e >> 1], (n - 1, 0)[e & 1]
        face[4 * n + e : 4 * n + e + 1] = res[k, j : j + 1]
    xp[:, :main] = data.T
    xp[:, main:] = face[...].T
    for i in range(1, 13):
        fetch(i).wait()
    wxm = split(dot3(hatx, split(v_stream[...])))
    amat = pick(is_m, dot3(split(v_span[...].T), split(at_z)))
    amat = amat * pick(is_n, dot3(split(v_normal[...].T), split(at_y)))
    a_h, a_l = split(amat)
    a_tri = jnp.concatenate([a_h, a_l, a_h], axis=1)
    wx_two = jnp.concatenate(wxm, axis=1)
    o = dg(hyz_two, d_split[0], (1, 0))
    o = o[:16] + (o[16:] + dg(hyz[0], d_split[1], (1, 0)))
    o = dg(jnp.concatenate(split(o), axis=0), wx_two, (1, 0))
    l_h, l_l = split(o[:16, :nm] + (o[:16, nm:] + o[16:, :nm]))
    mine[0, :, :nm] = dg(a_tri, jnp.concatenate([l_h, l_h, l_l], axis=0), (1, 0))

    pl.semaphore_wait(barrier, greeted)
    start(halos)
    start(lambda dy: planes(xp, (0, length - 1), xg, (0, 8), xr, 2, dy))
    begin(0)

    row, col = iota((rows, block), 0), iota((rows, block), 1)
    low = row & (n - 1)
    e0 = row - edge
    rk = jnp.where(row < main, (row >> sh) + 1, low + 1)
    rk = jnp.where((row >= main) & (row < main + n), 0, rk)
    rk = jnp.where((row >= main + n) & (row < main + 2 * n), n + 1, rk)
    rk = jnp.where(row >= edge, jnp.where(e0 < 2, 0, n + 1), rk)
    rk = jnp.where(row >= edge + 4, -1, rk)
    rj = jnp.where((row >= main + 2 * n) & (row < main + 3 * n), 0, low + 1)
    rj = jnp.where((row >= main + 3 * n) & (row < main + 4 * n), n + 1, rj)
    rj = jnp.where(row >= edge, jnp.where((e0 & 1) == 0, 0, n + 1), rj)
    rj = jnp.where(row >= edge + 4, -1, rj)
    sel_k, sel_j = onehot(rk == col), onehot(rj == col)
    brow, bcol = iota((block, lanes), 0), iota((block, lanes), 1)
    bq = quotient(bcol, block)
    to_r = onehot(bq == brow)
    to_q = onehot((bcol - block * bq == brow) & (bcol < block * block))
    span_l = dot3(split(span[...]), split(to_r))
    normal_l = dot3(split(normal[...].reshape(block, block)), split(to_q))
    kmat = pick(sel_k, span_l) * pick(sel_j, normal_l)
    k_hi, k_lo = split(kmat)
    kh[...] = k_hi
    kl[...] = k_lo
    wide = rows - main
    kf[...] = kmat[main : main + nrim]
    k3[0:wide] = k_hi[main:]
    k3[wide : 2 * wide] = k_hi[main:]
    k3[2 * wide :] = k_lo[main:]
    t_hi, t_lo = split(kmat.T)
    kth[...] = t_hi
    ktl[...] = t_lo
    k_main = kh[0:main], kl[0:main]

    nep = length + 16
    pairs = ne * block
    npad = -(-pairs // 16) * 16

    def place(c):
        far = jnp.where(c == length + 8, length, -n * length)
        return jnp.where(c < length, c, jnp.where(c == length, -1, far))

    wrow, wcol = iota((npad, nep), 0), iota((npad, nep), 1)
    xi = place(wcol) + 1 - n * quotient(wrow, block)
    trow, tcol = iota((block, nep), 0), iota((block, nep), 1)
    tx = place(tcol)
    tm = (tx + 1) & (n - 1)
    s_t = split(stream[...].T)
    first = dot3(s_t, split(onehot(trow == tm)))
    second = dot3(s_t, split(onehot(trow - n == tm)))
    prow, pcol = iota((npad, block), 0), iota((npad, block), 1)
    is_p = onehot((prow - block * quotient(prow, block) == pcol) & (prow < pairs))
    wmat = jnp.where((xi >= 0) & (xi < n), pick(is_p, first), 0.0)
    wmat = wmat + jnp.where((xi >= n) & (xi < block), pick(is_p, second), 0.0)
    w_h, w_l = split(wmat[:, :length])
    w_in = jnp.concatenate([w_h, ends], axis=0), jnp.concatenate([w_l, jnp.zeros_like(ends)], axis=0)
    w_two = jnp.concatenate(w_in, axis=0)
    nin = npad + 16
    w_back = split(wmat.T)
    eig_yz = dot3(split(jnp.broadcast_to(eig_z[...], (8, block))), split(to_r))
    eig_yz = eig_yz + dot3(split(jnp.broadcast_to(eig_y[...], (8, block))), split(to_q))
    ecol = jnp.sum(is_p * eig_x[...], axis=1, keepdims=True)
    ecol = jnp.where(iota((npad, 1), 0) < pairs, ecol, 1.0)
    inverse = 1.0 / (ecol + eig_yz[0:1])
    from_left = dot3(w_back, split(wmat[:, length : length + 1] * inverse))
    from_right = dot3(w_back, split(wmat[:, length + 8 : length + 9] * inverse))
    own_left = from_left[length : length + 1]
    own_right = from_right[length + 8 : length + 9]
    level = jnp.sum(is_m * lev_z[...], axis=1, keepdims=True)
    level = level + jnp.sum(is_n * lev_y[...], axis=1, keepdims=True) + lev_x[...]
    srow, slane = iota((8, rows - main), 0), iota((8, rows - main), 1)
    came = jnp.zeros(srow.shape, F32)
    went = jnp.zeros(srow.shape, F32)
    for s, (dz, dy) in enumerate(DIRS):
        at, number = span_of(dz, dy)
        came = jnp.where((srow == s) & (slane >= at) & (slane < at + number), 1.0, came)
        at, number = span_of(-dz, -dy)
        went = jnp.where((srow == s) & (slane >= at) & (slane < at + number), 1.0, went)
    part = dot3(split(dot3(w_in, d_split, (1, 1))), k_main)

    for side, turn in enumerate((from_left, from_right)):
        f_h, f_l = split(turn[:length])
        for third, half in enumerate((f_h, f_h, f_l)):
            f3[third * length : (third + 1) * length, side * lanes : (side + 1) * lanes] = half
        ghost = part[:npad] * inverse * wmat[:, length + 8 * side : length + 8 * side + 1]
        v0[8 * side : 8 * side + 1] = jnp.sum(ghost, axis=0, keepdims=True)
    b_two = jnp.concatenate([w_back[0][:length], w_back[1][:length]], axis=0)
    sp_h, sp_l = split(dot3(hyz, split(amat), (0, 1)))
    spread = jnp.concatenate([sp_h, sp_l, sp_h], axis=1)
    wx_rows = jnp.concatenate(wxm, axis=0)

    received(0)
    rim_h, rim_l = split(rim[...])
    near = jnp.concatenate([rim_h[:nrim], rim_l[:nrim], rim_h[:nrim]], axis=1)
    seen = dg(near, f3[...], (1, 0))
    for side in range(2):
        at = slice(8 * side, 8 * side + 1)
        term = seen[:, side * lanes : (side + 1) * lanes] * kf[...]
        vv[at] = v0[at] + jnp.sum(term, axis=0, keepdims=True)
    o = dg(w_two, jnp.concatenate([rim_h, rim_l], axis=0), (1, 1))
    onto = o[:nin, :wide] + (o[:nin, wide:] + o[nin:, :wide])
    o_h, o_l = split(onto)
    tri = jnp.concatenate([o_h, o_l, o_h], axis=1)
    v_h, v_l = split(vv[...])
    o = dg(jnp.concatenate([v_h, v_l], axis=0), kth[...], (1, 0))
    gx[...] = o[:16] + (o[16:] + dg(v_h, ktl[...], (1, 0)))
    for k in range(len(groups) - 1):
        mine[k + 1] = gather(k)
        begin(k + 1)
    start(lambda dy: planes(gx, (0, 8), tg, (0, length - 1), gr, 3, dy))


    received(2)
    xg[0:1, main:] = jnp.sum(xr[0:8] * came, axis=0, keepdims=True)
    xg[8:9, main:] = jnp.sum(xr[8:16] * came, axis=0, keepdims=True)
    g_h, g_l = split(xg[...])
    o = dg(jnp.concatenate([g_h, g_l], axis=0), kh[...], (1, 0))
    hx = o[:16] + (o[16:] + dg(g_h, kl[...], (1, 0)))
    part = part + dg(tri, k3[...], (1, 0))
    m_h, m_l = split(part[:npad] * inverse)
    o = dg(b_two, m_h, (1, 0))
    us[...] = o[:length] + (o[length:] + dg(b_two[:length], m_l, (1, 0)))
    us[0:1] += own_right * part[npad : npad + 1]
    us[length - 1 : length] += own_left * part[npad + 8 : npad + 9]

    u = split(us[...] + from_left[:length] * hx[0:1] + from_right[:length] * hx[8:9])
    r_two = jnp.concatenate([kh[main : main + nrim], kl[main : main + nrim]], axis=0)
    o = dg(r_two, jnp.concatenate(u, axis=0), (1, 1))
    back[...] = o[:nrim, :length] + (o[:nrim, length:] + o[nrim:, :length])
    start(rets)
    result = dot3(k_main, u, (1, 1))

    s_h, s_l = split(gather(len(groups) - 1)[:, :nm] / level)
    both = jnp.concatenate([s_h.astype(F32), s_l.astype(F32)], axis=0).astype(BF16)
    o = dg(both, wx_rows, (1, 1))
    c_h, c_l = split(o[:mn, :length] + (o[:mn, length:] + o[mn:, :length]))
    c_h = c_h.astype(F32)
    three = jnp.concatenate([c_h, c_h, c_l.astype(F32)], axis=0).astype(BF16)
    result = result + dg(spread, three, (1, 0))

    for base in range(4):
        settle(ssem.at[0], base)
    for k in range(len(groups)):
        settle_parts(ssem.at[0], k)
    received(3)
    tg[0:1, main:] = jnp.sum(gr[0:8] * went, axis=0, keepdims=True)
    tg[length - 1 : length, main:] = jnp.sum(gr[8:16] * went, axis=0, keepdims=True)
    turned = tg[...].T
    out[...] = (result + turned[:main]).reshape(n, n, length)
    received(1)
    extra = got[...] + turned[main : main + nrim]
    out[n - 1] += extra[0:n]
    out[0] += extra[n : 2 * n]
    out[:, n - 1] += extra[2 * n : 3 * n]
    out[:, 0] += extra[3 * n : 4 * n]
    for e in range(4):
        k, j = (n - 1, 0)[e >> 1], (n - 1, 0)[e & 1]
        out[k, j : j + 1] += extra[4 * n + e : 4 * n + e + 1]


def per_device(sizes, residual, local_stream, local_normal, local_span, eigen_stream, eigen_normal,
               eigen_span, vertex_stream, vertex_normal, vertex_span, level_stream, level_normal,
               level_span):
    nx, ny, nz = sizes
    block = local_stream.shape[0]
    n = block - 2
    length = residual.shape[2]
    nrim = 4 * n + 16
    wide = n * n + -(-nrim // 128) * 128
    lanes = -(-block * block // 128) * 128
    mn = ny * nz
    peers = mn - 1 + nx - 1 if mn <= 16 else nx + ny + nz - 3
    args = (
        residual, local_stream, local_normal.transpose(1, 0, 2), local_span,
        eigen_stream.reshape(1, -1), eigen_normal, eigen_span.reshape(1, -1), vertex_stream,
        vertex_normal, vertex_span, level_stream.reshape(1, -1), level_normal.reshape(1, -1),
        level_span.reshape(1, -1),
    )
    return pl.pallas_call(
        functools.partial(kernel, sizes),
        out_shape=pltpu.VMEM(residual.shape, F32),
        in_specs=[pl.BlockSpec(memory_space=pltpu.HBM)] * 13,
        out_specs=pl.BlockSpec(memory_space=pltpu.VMEM),
        scratch_shapes=[
            pltpu.VMEM((wide - n * n, length), F32),
            pltpu.VMEM((nrim, length), F32),
            pltpu.VMEM((wide - n * n, length), F32),
            pltpu.VMEM((length, wide), F32),
            pltpu.VMEM((16, wide), F32),
            pltpu.VMEM((24, wide - n * n), F32),
            pltpu.VMEM((16, wide), F32),
            pltpu.VMEM((length, wide), F32),
            pltpu.VMEM((24, wide - n * n), F32),
            pltpu.VMEM((16, lanes), F32),
            pltpu.VMEM((16, lanes), F32),
            pltpu.VMEM((nrim, lanes), F32),
            pltpu.VMEM((3 * length, 2 * lanes), BF16),
            pltpu.VMEM((wide, lanes), BF16),
            pltpu.VMEM((wide, lanes), BF16),
            pltpu.VMEM((3 * (wide - n * n), lanes), BF16),
            pltpu.VMEM((lanes, wide), BF16),
            pltpu.VMEM((lanes, wide), BF16),
            pltpu.VMEM((length, lanes), F32),
            pltpu.VMEM((nrim, length), F32),
            pltpu.VMEM((3, mn, vertex_stream.shape[1]), F32),
            pltpu.VMEM((peers, mn, vertex_stream.shape[1]), F32),
            pltpu.SemaphoreType.DMA((1,)),
            pltpu.SemaphoreType.DMA((6 if mn <= 16 else 7,)),
        ] + [pltpu.VMEM(a.shape, F32) for a in args],
        compiler_params=pltpu.CompilerParams(
            collective_id=0, has_side_effects=True
        ),
    )(*args)


def solution(mesh):
    sizes = (mesh.shape["ex"], mesh.shape["ey"], mesh.shape["ez"])
    placed = (P("ez", "ey", "ex"), P(), P("ey", None, None), P(), P(), P("ey", None)) + (P(),) * 7
    return jax.shard_map(
        functools.partial(per_device, sizes), mesh=mesh, in_specs=placed,
        out_specs=P("ez", "ey", "ex"), check_vma=False,
    )
```

```python
import functools
import math

import jax
import jax.numpy as jnp
from jax import lax
from jax.experimental import pallas as pl
from jax.experimental.pallas import tpu as pltpu
from jax.sharding import PartitionSpec as P

F32 = jnp.float32
BF16 = jnp.bfloat16
I32 = jnp.int32
DIRS = ((1, 0), (-1, 0), (0, 1), (0, -1), (1, 1), (1, -1), (-1, 1), (-1, -1))


def iota(shape, dim):
    return lax.broadcasted_iota(I32, shape, dim)


def quotient(x, d):
    return (x * (65536 // d + 1)) >> 16


def onehot(mask):
    return jnp.where(mask, 1.0, 0.0).astype(F32)


def split(x):
    hi = x.astype(BF16)
    return hi, (x - hi.astype(F32)).astype(BF16)


def dg(a, b, dims):
    return lax.dot_general(a, b, ((dims[:1], dims[1:]), ((), ())), preferred_element_type=F32)


def dot3(a, b, dims=(1, 0)):
    (ah, al), (bh, bl) = a, b
    return dg(ah, bh, dims) + (dg(ah, bl, dims) + dg(al, bh, dims))


def pick(mask, values, dims=(1, 0)):
    hi, lo = split(values)
    mask = mask.astype(BF16)
    return dg(mask, hi, dims) + dg(mask, lo, dims)


def hat(index, points):
    out = jnp.zeros(index.shape, F32)
    for i in range(points):
        out = jnp.where(index == i, (1.0 - math.cos(math.pi * i / (points - 1))) / 2.0, out)
    return out


def kernel(sizes, *refs):
    inputs, out = refs[:13], refs[13]
    (
        rim, got, face, xp, xg, xr, gx, tg, gr, vv, v0, kf, f3, kh, kl, k3, kth, ktl, us, back, mine, parts,
        ssem, rsem, isem,
    ) = refs[14:39]
    held = refs[39:]
    (
        res, stream, normal, span, eig_x, eig_y, eig_z,
        v_stream, v_normal, v_span, lev_x, lev_y, lev_z,
    ) = held
    nx, ny, nz = sizes
    block = stream.shape[0]
    n = block - 2
    sh = n.bit_length() - 1
    length = res.shape[2]
    ne = length // n
    main = n * n
    edge = main + 4 * n
    nrim = got.shape[0]
    rows, lanes = kh.shape
    nv, nm = v_stream.shape
    mn = nz * ny
    ix, iy, iz = lax.axis_index("ex"), lax.axis_index("ey"), lax.axis_index("ez")

    def fetch(i):
        return pltpu.make_async_copy(inputs[i], held[i], isem.at[min(i, 1)])

    for ref in (rim, xg, xr.at[0:16], tg.at[0:8], tg.at[length - 8 : length], gr.at[0:16]):
        ref[...] = jnp.zeros(ref.shape, F32)

    def wrap(i, size):
        return lax.rem(i + size, size)

    def where(dx, dy, dz):
        at = {}
        if dx:
            at["ex"] = wrap(ix + dx, nx)
        if dy:
            at["ey"] = iy + dy
        if dz:
            at["ez"] = wrap(iz + dz, nz)
        return at

    def has(dy):
        return jnp.logical_and(iy + dy >= 0, iy + dy < ny)

    def by_y(fn):
        for dy in (-1, 1):
            pl.when(has(dy))(functools.partial(fn, dy))
        fn(0)

    barrier = pltpu.get_barrier_semaphore()

    def signal(at):
        pl.semaphore_signal(
            barrier, inc=1, device_id=at, device_id_type=pl.DeviceIdType.MESH
        )

    def greet(dy):
        for dx in (1, -1, 0):
            for dz in (1, -1, 0):
                if dx or dy or dz:
                    signal(where(dx, dy, dz))

    groups = (("ez", "ey"), ("ex",)) if mn <= 16 else (("ez",), ("ey",), ("ex",))

    def peers(axes):
        found = []
        for d in range(nz if "ez" in axes else 1):
            for f in range(ny if "ey" in axes else 1):
                for e in range(nx if "ex" in axes else 1):
                    at = {}
                    if d:
                        at["ez"] = lax.rem(iz + d, nz)
                    if f:
                        at["ey"] = lax.rem(iy + f, ny)
                    if e:
                        at["ex"] = lax.rem(ix + e, nx)
                    near = d in (0, 1, nz - 1) and e in (0, 1, nx - 1) and f < (2 if ny == 2 else 1)
                    if at:
                        found.append((at, near))
        return found

    fetch(0).start()
    by_y(greet)
    greeted = 8 + jnp.where(iy > 0, 9, 0) + jnp.where(iy < ny - 1, 9, 0)
    for axes in groups:
        for at, near in peers(axes):
            if not near:
                signal(at)
                greeted = greeted + 1

    for i in range(1, 13):
        fetch(i).start()

    def shipped(src, dst, slot, at):
        return pltpu.make_async_remote_copy(
            src_ref=src, dst_ref=dst, send_sem=ssem.at[0], recv_sem=rsem.at[slot],
            device_id=at, device_id_type=pl.DeviceIdType.MESH,
        )

    def span_of(dz, dy):
        if dy == 0:
            return (0 if dz > 0 else n), n
        if dz == 0:
            return (2 * n if dy > 0 else 3 * n), n
        return 4 * n + (0 if dz > 0 else 2) + (0 if dy > 0 else 1), 1

    def halo(s):
        dz, dy = DIRS[s]
        if dy == 0:
            src = res.at[n - 1 if dz > 0 else 0]
        elif dz == 0:
            src = res.at[:, n - 1 if dy > 0 else 0]
        else:
            src = res.at[n - 1 if dz > 0 else 0, pl.ds(n - 1 if dy > 0 else 0, 1)]
        at, number = span_of(dz, dy)
        return shipped(src, rim.at[pl.ds(at, number)], 0, where(0, dy, dz))

    def ret(s):
        dz, dy = DIRS[s]
        part = pl.ds(*span_of(-dz, -dy))
        return shipped(back.at[part], got.at[part], 1, where(0, dy, dz))

    def halos(dy):
        return [halo(s) for s in range(8) if DIRS[s][1] == dy]

    def rets(dy):
        return [ret(s) for s in range(8) if DIRS[s][1] == dy]

    def planes(src, near_rows, whole, whole_rows, rest, base, dy):
        copies = []
        for dx in (1, -1):
            side = 0 if dx > 0 else 1
            near, far = near_rows[1 - side], 8 * side
            for s, (dz, sy) in enumerate(DIRS):
                if sy == dy:
                    copies.append(shipped(
                        src.at[pl.ds(near, 1), pl.ds(main, rows - main)],
                        rest.at[pl.ds(far + s, 1)], base, where(dx, dy, dz),
                    ))
            if dy == 0:
                copies.append(shipped(
                    src.at[pl.ds(near, 1), pl.ds(0, main)],
                    whole.at[pl.ds(whole_rows[side], 1), pl.ds(0, main)], base, where(dx, 0, 0),
                ))
        return copies

    def start(make):
        def go(dy):
            for c in make(dy):
                c.start()

        by_y(go)

    def take(sem, ref, count):
        bulk = ref.at[pl.ds(0, count)]
        pltpu.make_async_copy(bulk, bulk, sem).wait()

    amounts = (
        (rim, 2 * n, n + 2), (got, 2 * n, n + 2),
        (xr, 4 + 2 * main // (rows - main), 6), (gr, 4 + 2 * main // (rows - main), 6),
    )

    def settle(sem, base):
        ref, level, slope = amounts[base]
        if ny <= 2:
            take(sem, ref, level + slope * (ny - 1))
        else:
            inner = jnp.logical_and(has(1), has(-1))
            pl.when(inner)(lambda: take(sem, ref, level + 2 * slope))
            pl.when(jnp.logical_not(inner))(lambda: take(sem, ref, level + slope))

    def received(base):
        settle(rsem.at[base], base)

    def block_of(k):
        before = sum(len(peers(axes)) for axes in groups[:k])
        return before, len(peers(groups[k]))

    def begin(k):
        before, _ = block_of(k)
        for i, (at, _) in enumerate(peers(groups[k])):
            shipped(mine.at[k], parts.at[before + i], 4 + k, at).start()

    def settle_parts(sem, k):
        bulk = parts.at[pl.ds(*block_of(k))]
        pltpu.make_async_copy(bulk, bulk, sem).wait()

    def gather(k):
        before, count = block_of(k)
        settle_parts(rsem.at[4 + k], k)
        total = mine[k]
        for i in range(count):
            total = total + parts[before + i]
        return total

    hrow, hcol = iota((16, main), 0), iota((16, main), 1)
    wk, wj = hat(hcol >> sh, n), hat(hcol & (n - 1), n)
    hyz = jnp.where((hrow & 2) > 0, wk, 1.0 - wk) * jnp.where((hrow & 1) > 0, wj, 1.0 - wj)
    hyz = split(jnp.where(hrow < 4, hyz, 0.0))
    hyz_two = jnp.concatenate(hyz, axis=0)
    xrow, xcol = iota((length, nv), 0), iota((length, nv), 1)
    wx = hat(xrow & (n - 1), n)
    first_el = ix * ne + (xrow >> sh)
    after = jnp.where(first_el + 1 >= nv, first_el + 1 - nv, first_el + 1)
    hatx = jnp.where(xcol == first_el, 1.0 - wx, 0.0) + jnp.where(xcol == after, wx, 0.0)
    hatx = split(hatx)
    mrow, mcol = iota((mn, nz), 0), iota((mn, nz), 1)
    is_m = onehot((mrow >= mcol * ny) & (mrow < (mcol + 1) * ny))
    nrow, ncol = iota((mn, ny), 0), iota((mn, ny), 1)
    is_n = onehot(nrow - ny * quotient(nrow, ny) == ncol)
    vrow, vcol = iota((nz, 16), 0), iota((nz, 16), 1)
    vz = iz + (vcol >> 1)
    vz = jnp.where(vz >= nz, vz - nz, vz)
    at_z = onehot((vrow == vz) & (vcol < 4))
    urow, ucol = iota((ny, 16), 0), iota((ny, 16), 1)
    at_y = onehot((urow == iy + (ucol & 1)) & (ucol < 4))
    orow, ocol = iota((16, length), 0), iota((16, length), 1)
    ends = onehot(((orow == 0) & (ocol == 0)) | ((orow == 8) & (ocol == length - 1))).astype(BF16)
    face[...] = jnp.zeros_like(face)
    mine[...] = jnp.zeros_like(mine)
    vv[...] = jnp.zeros_like(vv)
    tg[8 : length - 8] = jnp.zeros((length - 16, rows), F32)

    got[...] = jnp.zeros_like(got)
    fetch(0).wait()
    data = res[...].reshape(main, length)
    d_split = split(data)
    face[0:n] = res[n - 1]
    face[n : 2 * n] = res[0]
    face[2 * n : 3 * n] = res[:, n - 1]
    face[3 * n : 4 * n] = res[:, 0]
    for e in range(4):
        k, j = (n - 1, 0)[e >> 1], (n - 1, 0)[e & 1]
        face[4 * n + e : 4 * n + e + 1] = res[k, j : j + 1]
    xp[:, :main] = data.T
    xp[:, main:] = face[...].T
    for i in range(1, 13):
        fetch(i).wait()
    wxm = split(dot3(hatx, split(v_stream[...])))
    amat = pick(is_m, dot3(split(v_span[...].T), split(at_z)))
    amat = amat * pick(is_n, dot3(split(v_normal[...].T), split(at_y)))
    a_h, a_l = split(amat)
    a_tri = jnp.concatenate([a_h, a_l, a_h], axis=1)
    wx_two = jnp.concatenate(wxm, axis=1)
    o = dg(hyz_two, d_split[0], (1, 0))
    o = o[:16] + (o[16:] + dg(hyz[0], d_split[1], (1, 0)))
    o = dg(jnp.concatenate(split(o), axis=0), wx_two, (1, 0))
    l_h, l_l = split(o[:16, :nm] + (o[:16, nm:] + o[16:, :nm]))
    mine[0, :, :nm] = dg(a_tri, jnp.concatenate([l_h, l_h, l_l], axis=0), (1, 0))

    pl.semaphore_wait(barrier, greeted)
    start(halos)
    start(lambda dy: planes(xp, (0, length - 1), xg, (0, 8), xr, 2, dy))
    begin(0)

    row, col = iota((rows, block), 0), iota((rows, block), 1)
    low = row & (n - 1)
    e0 = row - edge
    rk = jnp.where(row < main, (row >> sh) + 1, low + 1)
    rk = jnp.where((row >= main) & (row < main + n), 0, rk)
    rk = jnp.where((row >= main + n) & (row < main + 2 * n), n + 1, rk)
    rk = jnp.where(row >= edge, jnp.where(e0 < 2, 0, n + 1), rk)
    rk = jnp.where(row >= edge + 4, -1, rk)
    rj = jnp.where((row >= main + 2 * n) & (row < main + 3 * n), 0, low + 1)
    rj = jnp.where((row >= main + 3 * n) & (row < main + 4 * n), n + 1, rj)
    rj = jnp.where(row >= edge, jnp.where((e0 & 1) == 0, 0, n + 1), rj)
    rj = jnp.where(row >= edge + 4, -1, rj)
    sel_k, sel_j = onehot(rk == col), onehot(rj == col)
    brow, bcol = iota((block, lanes), 0), iota((block, lanes), 1)
    bq = quotient(bcol, block)
    to_r = onehot(bq == brow)
    to_q = onehot((bcol - block * bq == brow) & (bcol < block * block))
    span_l = dot3(split(span[...]), split(to_r))
    normal_l = dot3(split(normal[...].reshape(block, block)), split(to_q))
    kmat = pick(sel_k, span_l) * pick(sel_j, normal_l)
    k_hi, k_lo = split(kmat)
    kh[...] = k_hi
    kl[...] = k_lo
    wide = rows - main
    kf[...] = kmat[main : main + nrim]
    k3[0:wide] = k_hi[main:]
    k3[wide : 2 * wide] = k_hi[main:]
    k3[2 * wide :] = k_lo[main:]
    t_hi, t_lo = split(kmat.T)
    kth[...] = t_hi
    ktl[...] = t_lo
    k_main = kh[0:main], kl[0:main]

    nep = length + 16
    pairs = ne * block
    npad = -(-pairs // 16) * 16

    def place(c):
        far = jnp.where(c == length + 8, length, -n * length)
        return jnp.where(c < length, c, jnp.where(c == length, -1, far))

    wrow, wcol = iota((npad, nep), 0), iota((npad, nep), 1)
    xi = place(wcol) + 1 - n * quotient(wrow, block)
    trow, tcol = iota((block, nep), 0), iota((block, nep), 1)
    tx = place(tcol)
    tm = (tx + 1) & (n - 1)
    s_t = split(stream[...].T)
    first = dot3(s_t, split(onehot(trow == tm)))
    second = dot3(s_t, split(onehot(trow - n == tm)))
    prow, pcol = iota((npad, block), 0), iota((npad, block), 1)
    is_p = onehot((prow - block * quotient(prow, block) == pcol) & (prow < pairs))
    wmat = jnp.where((xi >= 0) & (xi < n), pick(is_p, first), 0.0)
    wmat = wmat + jnp.where((xi >= n) & (xi < block), pick(is_p, second), 0.0)
    w_h, w_l = split(wmat[:, :length])
    w_in = jnp.concatenate([w_h, ends], axis=0), jnp.concatenate([w_l, jnp.zeros_like(ends)], axis=0)
    w_two = jnp.concatenate(w_in, axis=0)
    nin = npad + 16
    w_back = split(wmat.T)
    eig_yz = dot3(split(jnp.broadcast_to(eig_z[...], (8, block))), split(to_r))
    eig_yz = eig_yz + dot3(split(jnp.broadcast_to(eig_y[...], (8, block))), split(to_q))
    ecol = jnp.sum(is_p * eig_x[...], axis=1, keepdims=True)
    ecol = jnp.where(iota((npad, 1), 0) < pairs, ecol, 1.0)
    inverse = 1.0 / (ecol + eig_yz[0:1])
    from_left = dot3(w_back, split(wmat[:, length : length + 1] * inverse))
    from_right = dot3(w_back, split(wmat[:, length + 8 : length + 9] * inverse))
    own_left = from_left[length : length + 1]
    own_right = from_right[length + 8 : length + 9]
    level = jnp.sum(is_m * lev_z[...], axis=1, keepdims=True)
    level = level + jnp.sum(is_n * lev_y[...], axis=1, keepdims=True) + lev_x[...]
    srow, slane = iota((8, rows - main), 0), iota((8, rows - main), 1)
    came = jnp.zeros(srow.shape, F32)
    went = jnp.zeros(srow.shape, F32)
    for s, (dz, dy) in enumerate(DIRS):
        at, number = span_of(dz, dy)
        came = jnp.where((srow == s) & (slane >= at) & (slane < at + number), 1.0, came)
        at, number = span_of(-dz, -dy)
        went = jnp.where((srow == s) & (slane >= at) & (slane < at + number), 1.0, went)
    part = dot3(split(dot3(w_in, d_split, (1, 1))), k_main)

    for side, turn in enumerate((from_left, from_right)):
        f_h, f_l = split(turn[:length])
        for third, half in enumerate((f_h, f_h, f_l)):
            f3[third * length : (third + 1) * length, side * lanes : (side + 1) * lanes] = half
        ghost = part[:npad] * inverse * wmat[:, length + 8 * side : length + 8 * side + 1]
        v0[8 * side : 8 * side + 1] = jnp.sum(ghost, axis=0, keepdims=True)
    b_two = jnp.concatenate([w_back[0][:length], w_back[1][:length]], axis=0)
    sp_h, sp_l = split(dot3(hyz, split(amat), (0, 1)))
    spread = jnp.concatenate([sp_h, sp_l, sp_h], axis=1)
    wx_rows = jnp.concatenate(wxm, axis=0)

    received(0)
    rim_h, rim_l = split(rim[...])
    near = jnp.concatenate([rim_h[:nrim], rim_l[:nrim], rim_h[:nrim]], axis=1)
    seen = dg(near, f3[...], (1, 0))
    for side in range(2):
        at = slice(8 * side, 8 * side + 1)
        term = seen[:, side * lanes : (side + 1) * lanes] * kf[...]
        vv[at] = v0[at] + jnp.sum(term, axis=0, keepdims=True)
    o = dg(w_two, jnp.concatenate([rim_h, rim_l], axis=0), (1, 1))
    onto = o[:nin, :wide] + (o[:nin, wide:] + o[nin:, :wide])
    o_h, o_l = split(onto)
    tri = jnp.concatenate([o_h, o_l, o_h], axis=1)
    v_h, v_l = split(vv[...])
    o = dg(jnp.concatenate([v_h, v_l], axis=0), kth[...], (1, 0))
    gx[...] = o[:16] + (o[16:] + dg(v_h, ktl[...], (1, 0)))
    start(lambda dy: planes(gx, (0, 8), tg, (0, length - 1), gr, 3, dy))

    for k in range(len(groups) - 1):
        mine[k + 1] = gather(k)
        begin(k + 1)

    received(2)
    xg[0:1, main:] = jnp.sum(xr[0:8] * came, axis=0, keepdims=True)
    xg[8:9, main:] = jnp.sum(xr[8:16] * came, axis=0, keepdims=True)
    g_h, g_l = split(xg[...])
    o = dg(jnp.concatenate([g_h, g_l], axis=0), kh[...], (1, 0))
    hx = o[:16] + (o[16:] + dg(g_h, kl[...], (1, 0)))
    part = part + dg(tri, k3[...], (1, 0))
    m_h, m_l = split(part[:npad] * inverse)
    o = dg(b_two, m_h, (1, 0))
    us[...] = o[:length] + (o[length:] + dg(b_two[:length], m_l, (1, 0)))
    us[0:1] += own_right * part[npad : npad + 1]
    us[length - 1 : length] += own_left * part[npad + 8 : npad + 9]

    u = split(us[...] + from_left[:length] * hx[0:1] + from_right[:length] * hx[8:9])
    r_two = jnp.concatenate([kh[main : main + nrim], kl[main : main + nrim]], axis=0)
    o = dg(r_two, jnp.concatenate(u, axis=0), (1, 1))
    back[...] = o[:nrim, :length] + (o[:nrim, length:] + o[nrim:, :length])
    start(rets)
    result = dot3(k_main, u, (1, 1))

    s_h, s_l = split(gather(len(groups) - 1)[:, :nm] / level)
    both = jnp.concatenate([s_h.astype(F32), s_l.astype(F32)], axis=0).astype(BF16)
    o = dg(both, wx_rows, (1, 1))
    c_h, c_l = split(o[:mn, :length] + (o[:mn, length:] + o[mn:, :length]))
    c_h = c_h.astype(F32)
    three = jnp.concatenate([c_h, c_h, c_l.astype(F32)], axis=0).astype(BF16)
    result = result + dg(spread, three, (1, 0))

    for base in range(4):
        settle(ssem.at[0], base)
    for k in range(len(groups)):
        settle_parts(ssem.at[0], k)
    received(3)
    tg[0:1, main:] = jnp.sum(gr[0:8] * went, axis=0, keepdims=True)
    tg[length - 1 : length, main:] = jnp.sum(gr[8:16] * went, axis=0, keepdims=True)
    turned = tg[...].T
    out[...] = (result + turned[:main]).reshape(n, n, length)
    received(1)
    extra = got[...] + turned[main : main + nrim]
    out[n - 1] += extra[0:n]
    out[0] += extra[n : 2 * n]
    out[:, n - 1] += extra[2 * n : 3 * n]
    out[:, 0] += extra[3 * n : 4 * n]
    for e in range(4):
        k, j = (n - 1, 0)[e >> 1], (n - 1, 0)[e & 1]
        out[k, j : j + 1] += extra[4 * n + e : 4 * n + e + 1]


def per_device(sizes, residual, local_stream, local_normal, local_span, eigen_stream, eigen_normal,
               eigen_span, vertex_stream, vertex_normal, vertex_span, level_stream, level_normal,
               level_span):
    nx, ny, nz = sizes
    block = local_stream.shape[0]
    n = block - 2
    length = residual.shape[2]
    nrim = 4 * n + 16
    wide = n * n + -(-nrim // 128) * 128
    lanes = -(-block * block // 128) * 128
    mn = ny * nz
    peers = mn - 1 + nx - 1 if mn <= 16 else nx + ny + nz - 3
    args = (
        residual, local_stream, local_normal.transpose(1, 0, 2), local_span,
        eigen_stream.reshape(1, -1), eigen_normal, eigen_span.reshape(1, -1), vertex_stream,
        vertex_normal, vertex_span, level_stream.reshape(1, -1), level_normal.reshape(1, -1),
        level_span.reshape(1, -1),
    )
    return pl.pallas_call(
        functools.partial(kernel, sizes),
        out_shape=pltpu.VMEM(residual.shape, F32),
        in_specs=[pl.BlockSpec(memory_space=pltpu.HBM)] * 13,
        out_specs=pl.BlockSpec(memory_space=pltpu.VMEM),
        scratch_shapes=[
            pltpu.VMEM((wide - n * n, length), F32),
            pltpu.VMEM((nrim, length), F32),
            pltpu.VMEM((wide - n * n, length), F32),
            pltpu.VMEM((length, wide), F32),
            pltpu.VMEM((16, wide), F32),
            pltpu.VMEM((24, wide - n * n), F32),
            pltpu.VMEM((16, wide), F32),
            pltpu.VMEM((length, wide), F32),
            pltpu.VMEM((24, wide - n * n), F32),
            pltpu.VMEM((16, lanes), F32),
            pltpu.VMEM((16, lanes), F32),
            pltpu.VMEM((nrim, lanes), F32),
            pltpu.VMEM((3 * length, 2 * lanes), BF16),
            pltpu.VMEM((wide, lanes), BF16),
            pltpu.VMEM((wide, lanes), BF16),
            pltpu.VMEM((3 * (wide - n * n), lanes), BF16),
            pltpu.VMEM((lanes, wide), BF16),
            pltpu.VMEM((lanes, wide), BF16),
            pltpu.VMEM((length, lanes), F32),
            pltpu.VMEM((nrim, length), F32),
            pltpu.VMEM((3, mn, vertex_stream.shape[1]), F32),
            pltpu.VMEM((peers, mn, vertex_stream.shape[1]), F32),
            pltpu.SemaphoreType.DMA((1,)),
            pltpu.SemaphoreType.DMA((6 if mn <= 16 else 7,)),
            pltpu.SemaphoreType.DMA((2,)),
        ] + [pltpu.VMEM(a.shape, F32) for a in args],
        compiler_params=pltpu.CompilerParams(
            collective_id=0, has_side_effects=True
        ),
    )(*args)


def solution(mesh):
    sizes = (mesh.shape["ex"], mesh.shape["ey"], mesh.shape["ez"])
    placed = (P("ez", "ey", "ex"), P(), P("ey", None, None), P(), P(), P("ey", None)) + (P(),) * 7
    return jax.shard_map(
        functools.partial(per_device, sizes), mesh=mesh, in_specs=placed,
        out_specs=P("ez", "ey", "ex"), check_vma=False,
    )
```
